512 devices in a mesh: gx: 16 (over z, x_lo), gy: 16 (over y, core), gz: 2 (over x_hi).
Axes of the slice: x: 4 (x_hi: 2, x_lo: 2; x = x_hi * 2 + x_lo), y: 8, z: 8, core: 2. Of those that a mesh axis runs over, the one named last changes fastest.
Arguments:
- tracers: float32 [5, 8, 2048, 2048], P(None, 'gz', 'gx', 'gy'), may hold values from 0 to 2
- wind_field: float32 [3, 8, 2048, 2048], P(None, 'gz', 'gx', 'gy'), may hold values from -0.2 to 0.2
- band_layer: int32 [2048, 2048], P('gx', 'gy'), may hold values from 0 to 6
- wall_mask: int32 [2048, 2048], P('gx', 'gy'), may hold values 0 or 1
- exit_mask: int32 [2048, 2048], P('gx', 'gy'), may hold values 0 or 1
- occupant_count: int32 [2048, 2048], P('gx', 'gy'), may hold values from 0 to 3
Outputs:
- tracers_out: float32 [5, 8, 2048, 2048], P(None, 'gz', 'gx', 'gy')
- occupants: float32 [2048, 2048], P('gx', 'gy')
- fed_density: float32 [2048, 2048], P('gx', 'gy')
The draws below stay inside these ranges and needn't reach their ends.
All inputs are finite; a program needn't handle non-finite values. No bound on the sum of `wall_mask` or of `exit_mask` on one device may be relied on, other than what follows from the above.
Results may differ from the reference program's by a relative error of at most 0.00002.
Values sent between devices are 32-bit elements; how exact they have to be, the bound alone decides.
A program may use at most 64 MiB of HBM per device.

```python
import jax
import jax.numpy as jnp

SPECIES = 5
SUBSTEPS = 2
CROWD_STEPS = 4
NX = 2048
NY = 2048
NZ = 8


def place_ends(values, key, smallest, largest):
    dims = values.shape
    spot = [jax.random.randint(jax.random.fold_in(key, axis), (), 0, dims[axis]) for axis in range(len(dims))]
    values = values.at[tuple(spot)].set(smallest)
    longest = dims.index(max(dims))
    spot[longest] = (spot[longest] + 1) % dims[longest]
    return values.at[tuple(spot)].set(largest)


def levels(own_key, dims, shards, low, top_value):
    factor_of, own = 1.0, jax.random.fold_in(own_key, 6)
    for axis_at, blocks in shards:
        draws = jnp.exp(jax.random.uniform(jax.random.fold_in(own, axis_at), (blocks,), jnp.float32, low / len(shards), top_value / len(shards)))
        factor_of = factor_of * jnp.repeat(draws, dims[axis_at] // blocks).reshape([-1 if axis == axis_at else 1 for axis in range(len(dims))])
    return factor_of


def setup_inputs(seed: int = 0) -> dict:
    streams_of = jax.random.split(jax.random.key(seed), 7)
    tracers = jnp.clip(2.0 * jax.random.uniform(streams_of[0], (SPECIES, NZ, NX, NY), jnp.float32) ** levels(streams_of[0], (SPECIES, NZ, NX, NY), ((1, 2), (2, 16), (3, 16)), -0.2, 0.2), 0.0, 2.0)
    wind_field = jnp.clip(jax.random.uniform(streams_of[1], (3, NZ, NX, NY), jnp.float32, -0.2, 0.2) * levels(streams_of[1], (3, NZ, NX, NY), ((1, 2), (2, 16), (3, 16)), -0.4, 0.0), -0.2, 0.2)
    band_layer = place_ends(jax.random.randint(streams_of[2], (NX, NY), 0, NZ - 1), jax.random.fold_in(streams_of[2], 1), 0, (NZ - 1) - 1).astype(jnp.int32)
    wall_mask = place_ends((jax.random.randint(streams_of[3], (NX, NY), 0, 8) < 1).astype(jnp.int32), jax.random.fold_in(streams_of[3], 1), 0, 1)
    exit_mask = place_ends((jax.random.randint(streams_of[4], (NX, NY), 0, 16) < 1).astype(jnp.int32), jax.random.fold_in(streams_of[4], 1), 0, 1)
    occupant_count = place_ends(jax.random.randint(streams_of[5], (NX, NY), 0, 4), jax.random.fold_in(streams_of[5], 1), 0, 3).astype(jnp.int32)
    return {"tracers": tracers, "wind_field": wind_field, "band_layer": band_layer, "wall_mask": wall_mask, "exit_mask": exit_mask, "occupant_count": occupant_count}


diffusivity = (0.05, 0.04, 0.06, 0.03, 0.045)


def advance(padded, wind):
    center = padded[:, 1:-1, 1:-1, 1:-1]
    z_lower = padded[:, :-2, 1:-1, 1:-1]
    z_upper = padded[:, 2:, 1:-1, 1:-1]
    x_lower = padded[:, 1:-1, :-2, 1:-1]
    x_upper = padded[:, 1:-1, 2:, 1:-1]
    y_lower = padded[:, 1:-1, 1:-1, :-2]
    y_upper = padded[:, 1:-1, 1:-1, 2:]
    laplace = x_lower + x_upper + y_lower + y_upper + z_lower + z_upper - 6.0 * center

    def upwind(velocity, lower, upper):
        return jnp.maximum(velocity, 0.0)[None] * (center - lower) + jnp.minimum(velocity, 0.0)[None] * (upper - center)

    transport = upwind(wind[0], x_lower, x_upper) + upwind(wind[1], y_lower, y_upper) + upwind(wind[2], z_lower, z_upper)
    coefficient = jnp.array(diffusivity, jnp.float32)[:, None, None, None]
    return center + coefficient * laplace - transport


def toxic_rate(exposure):
    return 0.3 * exposure[0] * jnp.exp(0.3 * exposure[1]) + 0.2 * exposure[2] + 0.1 * (2.0 - exposure[3]) ** 2 + 0.1 * exposure[4] ** 2


def crowd_step(occupants_pad, dose_pad, passable_pad, dose_rate, exit_share):
    occupants_mid = occupants_pad[1:-1, 1:-1]
    dose_mid = dose_pad[1:-1, 1:-1]
    gate_x = 0.25 * passable_pad[:-1, 1:-1] * passable_pad[1:, 1:-1] * (1.0 - occupants_pad[1:, 1:-1])
    carry_x = gate_x * occupants_pad[:-1, 1:-1]
    dose_x = gate_x * dose_pad[:-1, 1:-1]
    gate_y = 0.15 * passable_pad[1:-1, :-1] * passable_pad[1:-1, 1:] * (1.0 - occupants_pad[1:-1, 1:])
    carry_y = gate_y * occupants_pad[1:-1, :-1]
    dose_y = gate_y * dose_pad[1:-1, :-1]
    retain = 1.0 - 0.5 * exit_share
    occupants_new = (occupants_mid + carry_x[:-1] - carry_x[1:] + carry_y[:, :-1] - carry_y[:, 1:]) * retain
    dose_new = (dose_mid + dose_x[:-1] - dose_x[1:] + dose_y[:, :-1] - dose_y[:, 1:] + dose_rate * occupants_mid) * retain
    return occupants_new, dose_new


def reference(tracers, wind_field, band_layer, wall_mask, exit_mask, occupant_count):
    fields = tracers
    for step in range(SUBSTEPS):
        fields = advance(jnp.pad(fields, ((0, 0), (1, 1), (1, 1), (1, 1))), wind_field)
    layers = jnp.arange(NZ).astype(jnp.int32)[:, None, None]
    weight = ((layers == band_layer[None]) | (layers == band_layer[None] + 1)).astype(jnp.float32)
    exposure = 0.5 * jnp.sum(fields * weight[None], axis=1)
    dose_rate = toxic_rate(exposure)
    passable = 1.0 - wall_mask.astype(jnp.float32)
    exit_share = exit_mask.astype(jnp.float32)
    occupants = 0.25 * occupant_count.astype(jnp.float32) * passable
    dose = jnp.zeros_like(occupants)
    passable_pad = jnp.pad(passable, 1)
    for step in range(CROWD_STEPS):
        occupants, dose = crowd_step(jnp.pad(occupants, 1), jnp.pad(dose, 1), passable_pad, dose_rate, exit_share)
    return fields, occupants, dose
```

```python
import jax
import jax.numpy as jnp
from jax import lax
from jax.experimental import pallas as pl
from jax.experimental.pallas import tpu as pltpu
from jax.sharding import PartitionSpec as P

diffusivity = (0.05, 0.04, 0.06, 0.03, 0.045)
SPECIES = 5
L = 4
N = 128
CHUNK = 32
MESH = pl.DeviceIdType.MESH
f32 = jnp.float32


def coefficient_of(s):
    k = jnp.float32(diffusivity[0])
    for i in range(1, SPECIES):
        k = jnp.where(s == i, jnp.float32(diffusivity[i]), k)
    return k


def make_kernel(sizes):
    nx, ny, nz = sizes

    def kernel(
        tracers, wind, band_in, wall_in, exit_in, count_in,
        out_t, out_o, out_f,
        t0, t1, t2, wv, band, floor,
        ylo, yhi, ypack,
        xs, xr, ys, yr,
        m, c0, cx, cy, co,
        e_own, e_oth, er, es, ec, ed,
        sem_t, sem_w, sem_b, sem_f, sem_o,
        z_s, z_r, x_s, x_r, y_s, y_r, m_s, m_r,
        e_s, e_r, er_s, er_r, ec_s, ec_r,
    ):
        gx, gy, gz = lax.axis_index("gx"), lax.axis_index("gy"), lax.axis_index("gz")
        oz = 1 - gz
        gxn, gxp = lax.rem(gx + 1, nx), lax.rem(gx + nx - 1, nx)
        gyn, gyp = lax.rem(gy + 1, ny), lax.rem(gy + ny - 1, ny)
        boundary = (L - 1) * oz

        def layer_of(l):
            return l * oz + (L - 1 - l) * gz

        loads_t = [
            pltpu.make_async_copy(
                tracers.at[:, layer_of(l)], t0.at[:, l + 1, pl.ds(8, N), :], sem_t.at[l]
            )
            for l in range(L)
        ]
        loads_w = [
            pltpu.make_async_copy(wind.at[:, layer_of(l)], wv.at[:, l], sem_w.at[l])
            for l in range(L)
        ]
        loads_f = [
            pltpu.make_async_copy(ref, floor.at[i], sem_f.at[i])
            for i, ref in enumerate((wall_in, exit_in, count_in))
        ]
        load_b = pltpu.make_async_copy(band_in, band, sem_b)
        for c in loads_t:
            c.start()
        for c in loads_f:
            c.start()
        for c in loads_w:
            c.start()
        load_b.start()

        barrier = pltpu.get_barrier_semaphore()
        for dev in (
            (gx, gy, oz), (gxn, gy, gz), (gxp, gy, gz), (gx, gyn, gz), (gx, gyp, gz),
            (gxp, gy, oz), (gx, gyp, oz), (gxp, gyp, gz), (gxp, gyp, oz),
        ):
            pl.semaphore_signal(barrier, inc=1, device_id=dev, device_id_type=MESH)

        def clear(s, carry):
            t0[s, 0, pl.ds(8, N), :] = jnp.zeros((N, N), f32)
            t1[s, 0, pl.ds(8, N), :] = jnp.zeros((N, N), f32)
            return carry

        lax.fori_loop(0, SPECIES, clear, 0)
        pl.semaphore_wait(barrier, 9)

        def z_copy(step, s):
            src = tracers.at[s, boundary] if step == 0 else t1.at[s, L, pl.ds(8, N), :]
            dst = (t0 if step == 0 else t1).at[s, L + 1, pl.ds(8, N), :]
            return pltpu.make_async_remote_copy(
                src, dst, z_s.at[step, s], z_r.at[step, s],
                device_id=(gx, gy, oz), device_id_type=MESH,
            )

        def x_copy(step, d):
            return pltpu.make_async_remote_copy(
                xs.at[step, d], xr.at[step, d], x_s.at[step, d], x_r.at[step, d],
                device_id=((gxn if d == 0 else gxp), gy, gz), device_id_type=MESH,
            )

        def y_copy(step, d):
            return pltpu.make_async_remote_copy(
                ys.at[step, d], yr.at[step, d], y_s.at[step, d], y_r.at[step, d],
                device_id=(gx, (gyn if d == 0 else gyp), gz), device_id_type=MESH,
            )

        def m_copy(d):
            src, dst = ((N, 0), (8, N + 8))[d]
            return pltpu.make_async_remote_copy(
                m.at[:, :, pl.ds(src, 8), :], m.at[:, :, pl.ds(dst, 8), :],
                m_s.at[d], m_r.at[d],
                device_id=((gxn if d == 0 else gxp), gy, gz), device_id_type=MESH,
            )

        def e_copy(s):
            return pltpu.make_async_remote_copy(
                e_own.at[s], e_oth.at[s], e_s.at[s], e_r.at[s],
                device_id=(gx, gy, oz), device_id_type=MESH,
            )

        def er_copy(s, d):
            return pltpu.make_async_remote_copy(
                e_own.at[s, pl.ds(N - 8, 8), :], er.at[d, s],
                er_s.at[d, s], er_r.at[d, s],
                device_id=(gxn, gy, (gz if d == 0 else oz)), device_id_type=MESH,
            )

        def ec_copy(i):
            dev = ((gx, gyn, gz), (gx, gyn, oz), (gxn, gyn, gz), (gxn, gyn, oz))[i]
            return pltpu.make_async_remote_copy(
                es, ec.at[i], ec_s.at[i], ec_r.at[i], device_id=dev, device_id_type=MESH
            )

        z_copy(0, 0).start()
        z_copy(0, 1).start()

        lane = lax.broadcasted_iota(jnp.int32, (CHUNK, N), 1)
        chunks = tuple(range(0, N, CHUNK))

        def pack_x(src, step, s):
            for l in range(L):
                j = s * L + l
                xs[step, 0, pl.ds(j, 1), :] = src[s, l + 1, pl.ds(N + 7, 1), :]
                xs[step, 1, pl.ds(j, 1), :] = src[s, l + 1, pl.ds(8, 1), :]

        def pack_y(src, s):
            for r in chunks:
                low = ypack[0, pl.ds(r, CHUNK), :]
                high = ypack[1, pl.ds(r, CHUNK), :]
                for l in range(L):
                    j = s * L + l
                    c = src[s, l + 1, pl.ds(8 + r, CHUNK), :]
                    low = jnp.where(lane == j, pltpu.roll(c, j + 1, 1), low)
                    high = jnp.where(lane == j, pltpu.roll(c, j, 1), high)
                ypack[0, pl.ds(r, CHUNK), :] = low
                ypack[1, pl.ds(r, CHUNK), :] = high

        def unpack_x(dst, step):
            keep_low = (gx > 0).astype(f32)
            keep_high = (gx < nx - 1).astype(f32)
            for s in range(SPECIES):
                for l in range(L):
                    j = s * L + l
                    dst[s, l + 1, pl.ds(7, 1), :] = xr[step, 0, pl.ds(j, 1), :] * keep_low
                    dst[s, l + 1, pl.ds(N + 8, 1), :] = xr[step, 1, pl.ds(j, 1), :] * keep_high

        def unpack_y(step):
            keep_low = (gy > 0).astype(f32)
            keep_high = (gy < ny - 1).astype(f32)
            filler = jnp.zeros((N - 32, N), f32)
            ylo[...] = jnp.concatenate([yr[step, 0] * keep_low, filler], axis=0).T
            yhi[...] = jnp.concatenate([yr[step, 1] * keep_high, filler], axis=0).T

        def send_y(step):
            ys[step, 0] = ypack[0].T[:32]
            ys[step, 1] = ypack[1].T[:32]
            y_copy(step, 0).start()
            y_copy(step, 1).start()

        flip = (1 - 2 * gz).astype(f32)

        def moved(src, s, l, r, k):
            j = s * L + l
            c = src[s, l + 1, pl.ds(8 + r, CHUNK), :]
            total = c
            u = wv[0, l, pl.ds(r, CHUNK), :]
            total += (k + jnp.maximum(u, 0.0)) * (src[s, l + 1, pl.ds(7 + r, CHUNK), :] - c)
            total += (k - jnp.minimum(u, 0.0)) * (src[s, l + 1, pl.ds(9 + r, CHUNK), :] - c)
            u = wv[1, l, pl.ds(r, CHUNK), :]
            lower = jnp.where(
                lane == 0, pltpu.roll(ylo[pl.ds(r, CHUNK), :], N - j, 1), pltpu.roll(c, 1, 1)
            )
            upper = jnp.where(
                lane == N - 1, pltpu.roll(yhi[pl.ds(r, CHUNK), :], N - 1 - j, 1),
                pltpu.roll(c, N - 1, 1),
            )
            total += (k + jnp.maximum(u, 0.0)) * (lower - c)
            total += (k - jnp.minimum(u, 0.0)) * (upper - c)
            u = wv[2, l, pl.ds(r, CHUNK), :] * flip
            total += (k + jnp.maximum(u, 0.0)) * (src[s, l, pl.ds(8 + r, CHUNK), :] - c)
            total += (k - jnp.minimum(u, 0.0)) * (src[s, l + 2, pl.ds(8 + r, CHUNK), :] - c)
            return total

        for c in loads_t:
            c.wait()
        for s in range(SPECIES):
            pack_x(t0, 0, s)
        x_copy(0, 0).start()
        x_copy(0, 1).start()
        for s in range(2, SPECIES):
            z_copy(0, s).start()
        for c in loads_f:
            c.wait()
        passable = 1.0 - floor[0].astype(f32)
        leave = 1.0 - 0.5 * floor[1].astype(f32)
        start = 0.25 * floor[2].astype(f32) * passable
        m[0, 0, pl.ds(8, N), :] = start
        m[1, 0, pl.ds(8, N), :] = passable
        m[2, 0, pl.ds(8, N), :] = leave
        wide = lax.broadcasted_iota(jnp.int32, (N, N), 1)
        low = jnp.zeros((N, N), f32)
        high = jnp.zeros((N, N), f32)
        for i, field in enumerate((start, passable, leave)):
            a = 20 + 4 * i
            inside = (wide >= a) & (wide < a + 4)
            low = jnp.where(inside, pltpu.roll(field, a + 4, 1), low)
            high = jnp.where(inside, pltpu.roll(field, a, 1), high)
        ypack[0] = low
        ypack[1] = high

        def pack_y0(s, carry):
            pack_y(t0, s)
            return carry

        lax.fori_loop(0, SPECIES, pack_y0, 0)
        send_y(0)
        for c in loads_w:
            c.wait()
        load_b.wait()
        x_copy(0, 0).wait_recv()
        x_copy(0, 1).wait_recv()
        unpack_x(t0, 0)
        y_copy(0, 0).wait_recv()
        y_copy(0, 1).wait_recv()
        unpack_y(0)

        for i in range(3):
            a = 20 + 4 * i
            above = pltpu.roll(yhi[...], N - a, 1)
            below = pltpu.roll(ylo[...], N - 4 - a, 1)
            m[i, 1, pl.ds(8, N), :] = jnp.where(
                wide < 4, above, jnp.where(wide >= N - 4, below, 0.0)
            )
        m_copy(0).start()
        m_copy(1).start()

        def first(s, carry):
            k = coefficient_of(s)
            z_copy(0, s).wait_recv()
            for l in (L - 1, 0, 1, 2):
                for r in chunks:
                    t1[s, l + 1, pl.ds(8 + r, CHUNK), :] = moved(t0, s, l, r, k)
            z_copy(1, s).start()
            pack_x(t1, 1, s)
            pack_y(t1, s)
            return carry

        lax.fori_loop(0, SPECIES, first, 0)
        x_copy(1, 0).start()
        x_copy(1, 1).start()
        send_y(1)

        m_copy(0).wait()
        m_copy(1).wait()
        rows = N + 16
        lane_m = lax.broadcasted_iota(jnp.int32, (rows, N), 1)
        row_m = lax.broadcasted_iota(jnp.int32, (rows, N), 0)
        first_row = jnp.where(gx > 0, 0, 8)
        last_row = jnp.where(gx < nx - 1, rows, N + 8)
        inside = (row_m >= first_row) & (row_m < last_row)

        def y_lower(a, b):
            ra, rb = pltpu.roll(a, 1, 1), pltpu.roll(b, 1, 1)
            return jnp.where(lane_m == 0, rb, ra), jnp.where(lane_m == 0, ra, rb)

        def y_upper(a, b):
            ra, rb = pltpu.roll(a, N - 1, 1), pltpu.roll(b, N - 1, 1)
            return jnp.where(lane_m == N - 1, rb, ra), jnp.where(lane_m == N - 1, ra, rb)

        occ = [jnp.where(inside, m[0, i], 0.0) for i in range(2)]
        free = [jnp.where(inside, m[1, i], 0.0) for i in range(2)]
        out = [m[2, i] for i in range(2)]
        free_y = y_upper(*free)
        px = [0.25 * free[i] * pltpu.roll(free[i], rows - 1, 0) for i in range(2)]
        py = [0.15 * free[i] * free_y[i] for i in range(2)]
        for step in range(4):
            occ_yu = y_upper(*occ)
            occ_yl = y_lower(*occ)
            gate_x = [px[i] * (1.0 - pltpu.roll(occ[i], rows - 1, 0)) for i in range(2)]
            gate_y = [py[i] * (1.0 - occ_yu[i]) for i in range(2)]
            gate_yl = y_lower(*gate_y)
            after = []
            for i in range(2):
                stay = out[i] * (1.0 - gate_x[i] - gate_y[i])
                in_x = out[i] * pltpu.roll(gate_x[i], 1, 0)
                in_y = out[i] * gate_yl[i]
                c0[step, i] = stay[: N + 8]
                cx[step, i] = in_x[: N + 8]
                cy[step, i] = in_y[: N + 8]
                co[step, i] = (out[i] * occ[i])[: N + 8]
                after.append(stay * occ[i] + in_x * pltpu.roll(occ[i], 1, 0) + in_y * occ_yl[i])
            occ = after
        out_o[...] = occ[0][8 : N + 8]

        x_copy(1, 0).wait_recv()
        x_copy(1, 1).wait_recv()
        unpack_x(t1, 1)
        y_copy(1, 0).wait_recv()
        y_copy(1, 1).wait_recv()
        unpack_y(1)

        def out_copy(s, l):
            return pltpu.make_async_copy(t2.at[s, l], out_t.at[s, layer_of(l)], sem_o.at[s, l])

        def in_band(l, r):
            b = band[pl.ds(r, CHUNK), :]
            layer = l * oz + (2 * L - 1 - l) * gz
            return (b == layer) | (b == layer - 1)

        def second(s, carry):
            k = coefficient_of(s)
            for r in chunks:
                acc = jnp.zeros((CHUNK, N), f32)
                for l in range(L - 1):
                    new = moved(t1, s, l, r, k)
                    t2[s, l, pl.ds(r, CHUNK), :] = new
                    acc += jnp.where(in_band(l, r), 0.5 * new, 0.0)
                e_own[s, pl.ds(r, CHUNK), :] = acc
            z_copy(1, s).wait_recv()
            for r in chunks:
                new = moved(t1, s, L - 1, r, k)
                t2[s, L - 1, pl.ds(r, CHUNK), :] = new
                e_own[s, pl.ds(r, CHUNK), :] += jnp.where(in_band(L - 1, r), 0.5 * new, 0.0)
            for l in range(L):
                out_copy(s, l).start()
            er_copy(s, 0).start()
            er_copy(s, 1).start()
            e_copy(s).start()
            return carry

        lax.fori_loop(0, SPECIES, second, 0)
        strip = jnp.zeros((N, N), f32)
        for s in range(SPECIES):
            mine = (wide >= 3 * s) & (wide < 3 * s + 3)
            strip = jnp.where(mine, pltpu.roll(e_own[s], 3 * s + 3, 1), strip)
        es[...] = strip.T[:16]
        for i in range(4):
            ec_copy(i).start()

        def rate_of(co_, co2, hcn, o2, heat):
            return (
                0.3 * co_ * jnp.exp(0.3 * co2) + 0.2 * hcn
                + 0.1 * (2.0 - o2) * (2.0 - o2) + 0.1 * heat * heat
            )

        for s in range(SPECIES):
            er_copy(s, 0).wait_recv()
            er_copy(s, 1).wait_recv()
        edge = rate_of(*[er[0, s] + er[1, s] for s in range(SPECIES)])
        for i in range(4):
            ec_copy(i).wait_recv()
        filler = jnp.zeros((N - 16, N), f32)
        side = jnp.concatenate([ec[0] + ec[1], filler], axis=0).T
        corner = jnp.concatenate([ec[2] + ec[3], filler], axis=0).T[N - 8 :]
        side = jnp.concatenate([corner, side], axis=0)
        side = rate_of(*[pltpu.roll(side, N - 3 - 3 * s, 1) for s in range(SPECIES)])
        for s in range(SPECIES):
            e_copy(s).wait_recv()
        middle = rate_of(*[e_own[s] + e_oth[s] for s in range(SPECIES)])
        lane_d = lax.broadcasted_iota(jnp.int32, (N + 8, N), 1)
        rate = [
            jnp.concatenate([edge, middle], axis=0),
            jnp.where(lane_d >= N - 3, side, 0.0),
        ]
        dose = [co[0, i] * rate[i] for i in range(2)]
        for step in range(1, 4):
            ra, rb = pltpu.roll(dose[0], 1, 1), pltpu.roll(dose[1], 1, 1)
            left = (jnp.where(lane_d == 0, rb, ra), jnp.where(lane_d == 0, ra, rb))
            dose = [
                c0[step, i] * dose[i] + cx[step, i] * pltpu.roll(dose[i], 1, 0)
                + cy[step, i] * left[i] + co[step, i] * rate[i]
                for i in range(2)
            ]
        out_f[...] = dose[0][8:]

        for step in range(2):
            for d in range(2):
                x_copy(step, d).wait_send()
                y_copy(step, d).wait_send()

        def finish(s, carry):
            z_copy(0, s).wait_send()
            z_copy(1, s).wait_send()
            e_copy(s).wait_send()
            er_copy(s, 0).wait_send()
            er_copy(s, 1).wait_send()
            for l in range(L):
                out_copy(s, l).wait()
            return carry

        lax.fori_loop(0, SPECIES, finish, 0)
        for i in range(4):
            ec_copy(i).wait_send()

    return kernel


def solution(mesh):
    sizes = tuple(mesh.shape[name] for name in ("gx", "gy", "gz"))

    def on_device(tracers, wind_field, band_layer, wall_mask, exit_mask, occupant_count):
        floor = jax.ShapeDtypeStruct((N, N), f32)
        hbm = pl.BlockSpec(memory_space=pl.ANY)
        vmem = pl.BlockSpec(memory_space=pltpu.VMEM)
        V = pltpu.VMEM
        D = pltpu.SemaphoreType.DMA
        return pl.pallas_call(
            make_kernel(sizes),
            out_shape=(jax.ShapeDtypeStruct((SPECIES, L, N, N), f32), floor, floor),
            in_specs=[hbm] * 6,
            out_specs=(hbm, vmem, vmem),
            scratch_shapes=[
                V((SPECIES, L + 2, N + 16, N), f32),
                V((SPECIES, L + 2, N + 16, N), f32),
                V((SPECIES, L, N, N), f32),
                V((3, L, N, N), f32),
                V((N, N), jnp.int32),
                V((3, N, N), jnp.int32),
                V((N, N), f32), V((N, N), f32), V((2, N, N), f32),
                V((2, 2, 24, N), f32), V((2, 2, 24, N), f32),
                V((2, 2, 32, N), f32), V((2, 2, 32, N), f32),
                V((3, 2, N + 16, N), f32),
                V((4, 2, N + 8, N), f32), V((4, 2, N + 8, N), f32),
                V((4, 2, N + 8, N), f32), V((4, 2, N + 8, N), f32),
                V((SPECIES, N, N), f32), V((SPECIES, N, N), f32),
                V((2, SPECIES, 8, N), f32),
                V((16, N), f32), V((4, 16, N), f32), V((8, N), f32),
                D((L,)), D((L,)), D, D((3,)), D((SPECIES, L)),
                D((2, SPECIES)), D((2, SPECIES)),
                D((2, 2)), D((2, 2)), D((2, 2)), D((2, 2)), D((2,)), D((2,)),
                D((SPECIES,)), D((SPECIES,)), D((2, SPECIES)), D((2, SPECIES)),
                D((4,)), D((4,)),
            ],
            compiler_params=pltpu.CompilerParams(
                collective_id=0, has_side_effects=True, vmem_limit_bytes=48 * 1024 * 1024
            ),
        )(tracers, wind_field, band_layer, wall_mask, exit_mask, occupant_count)

    return jax.shard_map(
        on_device,
        mesh=mesh,
        in_specs=(
            P(None, "gz", "gx", "gy"),
            P(None, "gz", "gx", "gy"),
            P("gx", "gy"),
            P("gx", "gy"),
            P("gx", "gy"),
            P("gx", "gy"),
        ),
        out_specs=(P(None, "gz", "gx", "gy"), P("gx", "gy"), P("gx", "gy")),
        check_vma=False,
    )
```

```python
import jax
import jax.numpy as jnp
from jax import lax
from jax.experimental import pallas as pl
from jax.experimental.pallas import tpu as pltpu
from jax.sharding import PartitionSpec as P

diffusivity = (0.05, 0.04, 0.06, 0.03, 0.045)
SPECIES = 5
L = 4
N = 128
CHUNK = 32
HOLD = 3
MESH = pl.DeviceIdType.MESH
f32 = jnp.float32


def coefficient_of(s):
    k = jnp.float32(diffusivity[0])
    for i in range(1, SPECIES):
        k = jnp.where(s == i, jnp.float32(diffusivity[i]), k)
    return k


def make_kernel(sizes):
    nx, ny, nz = sizes

    def kernel(
        tracers, wind, band_in, wall_in, exit_in, count_in,
        out_t, out_o, out_f,
        t0, t1, wv, band, floor,
        yedge, ypack, ys, yr,
        m, c0, cx, cy, co,
        e_own, e_oth, er, es, ec,
        sem_t, sem_w, sem_b, sem_f,
        z_s, z_r, x_s, x_r, y_s, y_r, m_s, m_r,
        e_s, e_r, er_s, er_r, ec_s, ec_r,
    ):
        gx, gy, gz = lax.axis_index("gx"), lax.axis_index("gy"), lax.axis_index("gz")
        oz = 1 - gz
        gxn, gxp, gyn, gyp = gx + 1, gx - 1, gy + 1, gy - 1
        has_xn, has_xp, has_yn, has_yp = gx < nx - 1, gx > 0, gy < ny - 1, gy > 0
        x_has = (has_xn, has_xp)
        y_has = (has_yn, has_yp)
        boundary = (L - 1) * oz

        def layer_of(l):
            return l * oz + (L - 1 - l) * gz

        loads_t = [
            pltpu.make_async_copy(
                tracers.at[:, layer_of(l)], t0.at[:, l + 1, pl.ds(8, N), :], sem_t.at[l]
            )
            for l in range(L)
        ]
        loads_w = [
            pltpu.make_async_copy(wind.at[:, layer_of(l)], wv.at[:, l], sem_w.at[l])
            for l in range(L)
        ]
        loads_f = [
            pltpu.make_async_copy(ref, floor.at[i], sem_f.at[i])
            for i, ref in enumerate((wall_in, exit_in, count_in))
        ]
        load_b = pltpu.make_async_copy(band_in, band, sem_b)
        for c in loads_t:
            c.start()
        for c in loads_f:
            c.start()
        for c in loads_w:
            c.start()
        load_b.start()

        barrier = pltpu.get_barrier_semaphore()

        def greet(*devs):
            for dev in devs:
                pl.semaphore_signal(barrier, inc=1, device_id=dev, device_id_type=MESH)

        greet((gx, gy, oz))
        pl.when(has_xn)(lambda: greet((gxn, gy, gz)))
        pl.when(has_xp)(lambda: greet((gxp, gy, gz), (gxp, gy, oz)))
        pl.when(has_yn)(lambda: greet((gx, gyn, gz)))
        pl.when(has_yp)(lambda: greet((gx, gyp, gz), (gx, gyp, oz)))
        pl.when(has_xp & has_yp)(lambda: greet((gxp, gyp, gz), (gxp, gyp, oz)))

        def clear(s, carry):
            t0[s, 0, pl.ds(8, N), :] = jnp.zeros((N, N), f32)
            t1[s, 0, pl.ds(8, N), :] = jnp.zeros((N, N), f32)
            return carry

        lax.fori_loop(0, SPECIES, clear, 0)

        def clear_rows(row):
            for s in range(SPECIES):
                for l in range(1, L + 1):
                    t0[s, l, pl.ds(row, 1), :] = jnp.zeros((1, N), f32)
                    t1[s, l, pl.ds(row, 1), :] = jnp.zeros((1, N), f32)

        er[:, :, pl.ds(0, 5), :] = jnp.zeros((2, SPECIES, 5, N), f32)
        m[:, :, pl.ds(0, 4), :] = jnp.zeros((3, 2, 4, N), f32)
        m[:, :, pl.ds(N + 12, 4), :] = jnp.zeros((3, 2, 4, N), f32)

        @pl.when(jnp.logical_not(has_xp))
        def _():
            clear_rows(7)
            er[:, :, pl.ds(5, 3), :] = jnp.zeros((2, SPECIES, 3, N), f32)
            m[:, :, pl.ds(4, 4), :] = jnp.zeros((3, 2, 4, N), f32)

        @pl.when(jnp.logical_not(has_xn))
        def _():
            clear_rows(N + 8)
            m[:, :, pl.ds(N + 8, 4), :] = jnp.zeros((3, 2, 4, N), f32)

        @pl.when(jnp.logical_not(has_yp))
        def _():
            yr[0, 0] = jnp.zeros((72, N), f32)
            yr[1, 0] = jnp.zeros((72, N), f32)
            ec[0] = jnp.zeros((16, N), f32)
            ec[1] = jnp.zeros((16, N), f32)

        @pl.when(jnp.logical_not(has_yn))
        def _():
            yr[0, 1] = jnp.zeros((72, N), f32)
            yr[1, 1] = jnp.zeros((72, N), f32)

        @pl.when(jnp.logical_not(has_xp & has_yp))
        def _():
            ec[2] = jnp.zeros((16, N), f32)
            ec[3] = jnp.zeros((16, N), f32)

        one = lambda flag: flag.astype(jnp.int32)
        pl.semaphore_wait(
            barrier,
            1 + 2 * one(has_xn) + one(has_xp) + 2 * one(has_yn) + one(has_yp)
            + 2 * one(has_xn) * one(has_yn),
        )

        def z_copy(step, s):
            src = tracers.at[s, boundary] if step == 0 else t1.at[s, L, pl.ds(8, N), :]
            dst = (t0 if step == 0 else t1).at[s, L + 1, pl.ds(8, N), :]
            return pltpu.make_async_remote_copy(
                src, dst, z_s.at[step, s], z_r.at[step, s],
                device_id=(gx, gy, oz), device_id_type=MESH,
            )

        def x_copies(step, d):
            dev = ((gxn if d == 0 else gxp), gy, gz)
            src, dst = ((N + 7, 7), (8, N + 8))[d]
            if step == 1:
                return [
                    pltpu.make_async_remote_copy(
                        t1.at[:, pl.ds(1, L), pl.ds(src, 1), :],
                        t1.at[:, pl.ds(1, L), pl.ds(dst, 1), :],
                        x_s.at[1, d, 0], x_r.at[1, d, 0],
                        device_id=dev, device_id_type=MESH,
                    )
                ]
            return [
                pltpu.make_async_remote_copy(
                    tracers.at[:, layer_of(l), pl.ds(src - 8, 1), :],
                    t0.at[:, l + 1, pl.ds(dst, 1), :],
                    x_s.at[0, d, l], x_r.at[0, d, l],
                    device_id=dev, device_id_type=MESH,
                )
                for l in range(L)
            ]

        def y_copy(step, d):
            rows = 72 if step == 0 else 48
            return pltpu.make_async_remote_copy(
                ys.at[step, pl.ds(0, rows), :], yr.at[step, d, pl.ds(0, rows), :],
                y_s.at[step, d], y_r.at[step, d],
                device_id=(gx, (gyn if d == 0 else gyp), gz), device_id_type=MESH,
            )

        def m_copy(d):
            src, dst = ((N + 4, 4), (8, N + 8))[d]
            return pltpu.make_async_remote_copy(
                m.at[:, :, pl.ds(src, 4), :], m.at[:, :, pl.ds(dst, 4), :],
                m_s.at[d], m_r.at[d],
                device_id=((gxn if d == 0 else gxp), gy, gz), device_id_type=MESH,
            )

        def send_x(step):
            for d in range(2):
                @pl.when(x_has[d])
                def _():
                    for c in x_copies(step, d):
                        c.start()

        def recv_x(step):
            for d in range(2):
                @pl.when(x_has[1 - d])
                def _():
                    for c in x_copies(step, d):
                        c.wait_recv()

        def recv_y(step):
            for d in range(2):
                pl.when(y_has[1 - d])(lambda: y_copy(step, d).wait_recv())

        def e_copy(s):
            return pltpu.make_async_remote_copy(
                e_own.at[s], e_oth.at[s], e_s.at[s], e_r.at[s],
                device_id=(gx, gy, oz), device_id_type=MESH,
            )

        def er_copy(s, d):
            return pltpu.make_async_remote_copy(
                e_own.at[s, pl.ds(N - 3, 3), :], er.at[d, s, pl.ds(5, 3), :],
                er_s.at[d, s], er_r.at[d, s],
                device_id=(gxn, gy, (gz if d == 0 else oz)), device_id_type=MESH,
            )

        def ec_copy(i):
            dev = ((gx, gyn, gz), (gx, gyn, oz), (gxn, gyn, gz), (gxn, gyn, oz))[i]
            return pltpu.make_async_remote_copy(
                es, ec.at[i], ec_s.at[i], ec_r.at[i], device_id=dev, device_id_type=MESH
            )

        send_x(0)
        z_copy(0, 0).start()
        z_copy(0, 1).start()

        lane = lax.broadcasted_iota(jnp.int32, (CHUNK, N), 1)
        chunks = tuple(range(0, N, CHUNK))

        def pack_y(src, s):
            for r in chunks:
                acc = ypack[pl.ds(r, CHUNK), :]
                for l in range(L):
                    j = 2 * (s * L + l)
                    c = src[s, l + 1, pl.ds(8 + r, CHUNK), :]
                    here = (lane == j + 1) | (lane == j + 2)
                    acc = jnp.where(here, pltpu.roll(c, j + 2, 1), acc)
                ypack[pl.ds(r, CHUNK), :] = acc

        def unpack_y(step):
            row = lax.broadcasted_iota(jnp.int32, (72, N), 0)
            before = yr[step, 0]
            after = yr[step, 1]
            after = jnp.where(row < 48, pltpu.roll(after, 70, 0), after)
            from_before = ((row < 48) & ((row & 1) == 1)) | ((row >= 48) & ((row & 7) < 4))
            both = jnp.where(from_before, before, after)
            yedge[...] = jnp.concatenate([both, jnp.zeros((N - 72, N), f32)], axis=0).T

        def send_y(step):
            ys[step] = ypack[...].T[:72]
            for d in range(2):
                pl.when(y_has[d])(lambda: y_copy(step, d).start())

        flip = (1 - 2 * gz).astype(f32)

        def moved(src, s, l, r, k):
            j = s * L + l
            c = src[s, l + 1, pl.ds(8 + r, CHUNK), :]
            total = c
            u = wv[0, l, pl.ds(r, CHUNK), :]
            total += (k + jnp.maximum(u, 0.0)) * (src[s, l + 1, pl.ds(7 + r, CHUNK), :] - c)
            total += (k - jnp.minimum(u, 0.0)) * (src[s, l + 1, pl.ds(9 + r, CHUNK), :] - c)
            u = wv[1, l, pl.ds(r, CHUNK), :]
            edge = pltpu.roll(yedge[pl.ds(r, CHUNK), :], N - 1 - 2 * j, 1)
            lower = jnp.where(lane == 0, edge, pltpu.roll(c, 1, 1))
            upper = jnp.where(lane == N - 1, edge, pltpu.roll(c, N - 1, 1))
            total += (k + jnp.maximum(u, 0.0)) * (lower - c)
            total += (k - jnp.minimum(u, 0.0)) * (upper - c)
            u = wv[2, l, pl.ds(r, CHUNK), :] * flip
            total += (k + jnp.maximum(u, 0.0)) * (src[s, l, pl.ds(8 + r, CHUNK), :] - c)
            total += (k - jnp.minimum(u, 0.0)) * (src[s, l + 2, pl.ds(8 + r, CHUNK), :] - c)
            return total

        for c in loads_f:
            c.wait()
        passable = 1.0 - floor[0].astype(f32)
        leave = 1.0 - 0.5 * floor[1].astype(f32)
        start = 0.25 * floor[2].astype(f32) * passable
        m[0, 0, pl.ds(8, N), :] = start
        m[1, 0, pl.ds(8, N), :] = passable
        m[2, 0, pl.ds(8, N), :] = leave
        wide = lax.broadcasted_iota(jnp.int32, (N, N), 1)
        acc = jnp.zeros((N, N), f32)
        for i, field in enumerate((start, passable, leave)):
            a = 48 + 8 * i
            acc = jnp.where((wide >= a) & (wide < a + 8), pltpu.roll(field, a + 4, 1), acc)
        ypack[...] = acc
        for c in loads_t:
            c.wait()

        def pack_y0(s, carry):
            pack_y(t0, s)
            return carry

        lax.fori_loop(0, SPECIES, pack_y0, 0)
        send_y(0)
        for s in range(2, SPECIES):
            z_copy(0, s).start()
        for c in loads_w:
            c.wait()
        load_b.wait()
        recv_y(0)
        unpack_y(0)

        for i in range(3):
            beside = pltpu.roll(yedge[...], N - 52 - 8 * i, 1)
            m[i, 1, pl.ds(8, N), :] = jnp.where((wide < 4) | (wide >= N - 4), beside, 0.0)
        for d in range(2):
            pl.when(x_has[d])(lambda: m_copy(d).start())
        recv_x(0)

        def first(s, carry):
            k = coefficient_of(s)
            z_copy(0, s).wait_recv()
            for l in (L - 1, 0, 1, 2):
                for r in chunks:
                    t1[s, l + 1, pl.ds(8 + r, CHUNK), :] = moved(t0, s, l, r, k)

            @pl.when(s < 2)
            def _():
                z_copy(1, s).start()

            pack_y(t1, s)
            return carry

        lax.fori_loop(0, SPECIES, first, 0)
        send_x(1)
        send_y(1)
        for s in range(2, SPECIES):
            z_copy(1, s).start()

        for d in range(2):
            pl.when(x_has[1 - d])(lambda: m_copy(d).wait_recv())
        rows = N + 16
        lane_m = lax.broadcasted_iota(jnp.int32, (rows, N), 1)

        def y_lower(a, b):
            ra, rb = pltpu.roll(a, 1, 1), pltpu.roll(b, 1, 1)
            return jnp.where(lane_m == 0, rb, ra), jnp.where(lane_m == 0, ra, rb)

        def y_upper(a, b):
            ra, rb = pltpu.roll(a, N - 1, 1), pltpu.roll(b, N - 1, 1)
            return jnp.where(lane_m == N - 1, rb, ra), jnp.where(lane_m == N - 1, ra, rb)

        occ = [m[0, i] for i in range(2)]
        free = [m[1, i] for i in range(2)]
        out = [m[2, i] for i in range(2)]
        free_y = y_upper(*free)
        px = [0.25 * free[i] * pltpu.roll(free[i], rows - 1, 0) for i in range(2)]
        py = [0.15 * free[i] * free_y[i] for i in range(2)]
        for step in range(4):
            occ_yu = y_upper(*occ)
            occ_yl = y_lower(*occ)
            gate_x = [px[i] * (1.0 - pltpu.roll(occ[i], rows - 1, 0)) for i in range(2)]
            gate_y = [py[i] * (1.0 - occ_yu[i]) for i in range(2)]
            gate_yl = y_lower(*gate_y)
            after = []
            for i in range(2):
                stay = out[i] * (1.0 - gate_x[i] - gate_y[i])
                in_x = out[i] * pltpu.roll(gate_x[i], 1, 0)
                in_y = out[i] * gate_yl[i]
                c0[step, i] = stay[: N + 8]
                cx[step, i] = in_x[: N + 8]
                cy[step, i] = in_y[: N + 8]
                co[step, i] = (out[i] * occ[i])[: N + 8]
                after.append(stay * occ[i] + in_x * pltpu.roll(occ[i], 1, 0) + in_y * occ_yl[i])
            occ = after
        out_o[...] = occ[0][8 : N + 8]

        recv_x(1)
        recv_y(1)
        unpack_y(1)

        def in_band(l, r):
            b = band[pl.ds(r, CHUNK), :]
            layer = l * oz + (2 * L - 1 - l) * gz
            return (b == layer) | (b == layer - 1)

        def second(s, carry):
            k = coefficient_of(s)
            for r in chunks:
                acc = jnp.zeros((CHUNK, N), f32)
                for l in range(L - 1):
                    new = moved(t1, s, l, r, k)
                    out_t[s, layer_of(l), pl.ds(r, CHUNK), :] = new
                    acc += jnp.where(in_band(l, r), 0.5 * new, 0.0)
                e_own[s, pl.ds(r, CHUNK), :] = acc
            z_copy(1, s).wait_recv()
            for r in chunks:
                new = moved(t1, s, L - 1, r, k)
                out_t[s, boundary, pl.ds(r, CHUNK), :] = new
                e_own[s, pl.ds(r, CHUNK), :] += jnp.where(in_band(L - 1, r), 0.5 * new, 0.0)

            @pl.when(has_xn)
            def _():
                er_copy(s, 0).start()
                er_copy(s, 1).start()

            @pl.when(s < HOLD)
            def _():
                e_copy(s).start()

            return carry

        lax.fori_loop(0, SPECIES, second, 0)
        strip = jnp.zeros((N, N), f32)
        for s in range(SPECIES):
            mine = (wide >= 3 * s) & (wide < 3 * s + 3)
            strip = jnp.where(mine, pltpu.roll(e_own[s], 3 * s + 3, 1), strip)
        es[...] = strip.T[:16]
        ec_to = (has_yn, has_yn, has_xn & has_yn, has_xn & has_yn)
        ec_from = (has_yp, has_yp, has_xp & has_yp, has_xp & has_yp)
        for i in range(4):
            pl.when(ec_to[i])(lambda: ec_copy(i).start())
        for s in range(HOLD, SPECIES):
            e_copy(s).start()

        def rate_of(co_, co2, hcn, o2, heat):
            return (
                0.3 * co_ * jnp.exp(0.3 * co2) + 0.2 * hcn
                + 0.1 * (2.0 - o2) * (2.0 - o2) + 0.1 * heat * heat
            )

        @pl.when(has_xp)
        def _():
            for s in range(SPECIES):
                er_copy(s, 0).wait_recv()
                er_copy(s, 1).wait_recv()

        edge = rate_of(*[er[0, s] + er[1, s] for s in range(SPECIES)])
        for i in range(4):
            pl.when(ec_from[i])(lambda: ec_copy(i).wait_recv())
        filler = jnp.zeros((N - 16, N), f32)
        side = jnp.concatenate([ec[0] + ec[1], filler], axis=0).T
        corner = jnp.concatenate([ec[2] + ec[3], filler], axis=0).T[N - 8 :]
        side = jnp.concatenate([corner, side], axis=0)
        side = rate_of(*[pltpu.roll(side, N - 3 - 3 * s, 1) for s in range(SPECIES)])
        for s in range(SPECIES):
            e_copy(s).wait_recv()
        middle = rate_of(*[e_own[s] + e_oth[s] for s in range(SPECIES)])
        lane_d = lax.broadcasted_iota(jnp.int32, (N + 8, N), 1)
        rate = [
            jnp.concatenate([edge, middle], axis=0),
            jnp.where(lane_d >= N - 3, side, 0.0),
        ]
        dose = [co[0, i] * rate[i] for i in range(2)]
        for step in range(1, 4):
            ra, rb = pltpu.roll(dose[0], 1, 1), pltpu.roll(dose[1], 1, 1)
            left = (jnp.where(lane_d == 0, rb, ra), jnp.where(lane_d == 0, ra, rb))
            dose = [
                c0[step, i] * dose[i] + cx[step, i] * pltpu.roll(dose[i], 1, 0)
                + cy[step, i] * left[i] + co[step, i] * rate[i]
                for i in range(2)
            ]
        out_f[...] = dose[0][8:]

        for d in range(2):
            @pl.when(x_has[d])
            def _():
                for step in range(2):
                    for c in x_copies(step, d):
                        c.wait_send()
                m_copy(d).wait_send()

            @pl.when(y_has[d])
            def _():
                for step in range(2):
                    y_copy(step, d).wait_send()

        for s in range(SPECIES):
            z_copy(0, s).wait_send()
            z_copy(1, s).wait_send()
            e_copy(s).wait_send()

        @pl.when(has_xn)
        def _():
            for s in range(SPECIES):
                er_copy(s, 0).wait_send()
                er_copy(s, 1).wait_send()

        for i in range(4):
            pl.when(ec_to[i])(lambda: ec_copy(i).wait_send())

    return kernel


def solution(mesh):
    sizes = tuple(mesh.shape[name] for name in ("gx", "gy", "gz"))

    def on_device(tracers, wind_field, band_layer, wall_mask, exit_mask, occupant_count):
        floor = jax.ShapeDtypeStruct((N, N), f32)
        hbm = pl.BlockSpec(memory_space=pl.ANY)
        vmem = pl.BlockSpec(memory_space=pltpu.VMEM)
        V = pltpu.VMEM
        D = pltpu.SemaphoreType.DMA
        return pl.pallas_call(
            make_kernel(sizes),
            out_shape=(jax.ShapeDtypeStruct((SPECIES, L, N, N), f32), floor, floor),
            in_specs=[hbm] * 6,
            out_specs=(vmem, vmem, vmem),
            scratch_shapes=[
                V((SPECIES, L + 2, N + 16, N), f32),
                V((SPECIES, L + 2, N + 16, N), f32),
                V((3, L, N, N), f32),
                V((N, N), jnp.int32),
                V((3, N, N), jnp.int32),
                V((N, N), f32), V((N, N), f32),
                V((2, 72, N), f32), V((2, 2, 72, N), f32),
                V((3, 2, N + 16, N), f32),
                V((4, 2, N + 8, N), f32), V((4, 2, N + 8, N), f32),
                V((4, 2, N + 8, N), f32), V((4, 2, N + 8, N), f32),
                V((SPECIES, N, N), f32), V((SPECIES, N, N), f32),
                V((2, SPECIES, 8, N), f32),
                V((16, N), f32), V((4, 16, N), f32),
                D((L,)), D((L,)), D, D((3,)),
                D((2, SPECIES)), D((2, SPECIES)),
                D((2, 2, L)), D((2, 2, L)), D((2, 2)), D((2, 2)), D((2,)), D((2,)),
                D((SPECIES,)), D((SPECIES,)), D((2, SPECIES)), D((2, SPECIES)),
                D((4,)), D((4,)),
            ],
            compiler_params=pltpu.CompilerParams(
                collective_id=0, has_side_effects=True, vmem_limit_bytes=48 * 1024 * 1024
            ),
        )(*[pltpu.with_memory_space_constraint(a, pltpu.HBM) for a in (tracers, wind_field, band_layer, wall_mask, exit_mask, occupant_count)])

    return jax.shard_map(
        on_device,
        mesh=mesh,
        in_specs=(
            P(None, "gz", "gx", "gy"),
            P(None, "gz", "gx", "gy"),
            P("gx", "gy"),
            P("gx", "gy"),
            P("gx", "gy"),
            P("gx", "gy"),
        ),
        out_specs=(P(None, "gz", "gx", "gy"), P("gx", "gy"), P("gx", "gy")),
        check_vma=False,
    )
```

```python
import jax
import jax.numpy as jnp
from jax import lax
from jax.experimental import pallas as pl
from jax.experimental.pallas import tpu as pltpu
from jax.sharding import PartitionSpec as P

diffusivity = (0.05, 0.04, 0.06, 0.03, 0.045)
SPECIES = 5
L = 4
N = 128
CHUNK = 32
HOLD = 3
PARTS = ((0, 3), (3, 2))
EDGE_ROWS = ((0, 72), (0, 32), (24, 24))
MESH = pl.DeviceIdType.MESH
f32 = jnp.float32


def coefficient_of(s):
    k = jnp.float32(diffusivity[0])
    for i in range(1, SPECIES):
        k = jnp.where(s == i, jnp.float32(diffusivity[i]), k)
    return k


def make_kernel(sizes):
    nx, ny, nz = sizes

    def kernel(
        tracers, wind, band_in, wall_in, exit_in, count_in,
        out_t, out_o, c0, cx, cy, co, out_rate,
        t0, t1, wv, band, floor,
        yedge, ypack, ys, yr,
        m,
        e_own, e_oth, er, es, ec,
        sem_t, sem_w, sem_b, sem_f,
        z_s, z_r, x_s, x_r, y_s, y_r, m_s, m_r,
        e_s, e_r, er_s, er_r, ec_s, ec_r,
    ):
        gx, gy, gz = lax.axis_index("gx"), lax.axis_index("gy"), lax.axis_index("gz")
        oz = 1 - gz
        gxn, gxp, gyn, gyp = gx + 1, gx - 1, gy + 1, gy - 1
        has_xn, has_xp, has_yn, has_yp = gx < nx - 1, gx > 0, gy < ny - 1, gy > 0
        x_has = (has_xn, has_xp)
        y_has = (has_yn, has_yp)
        boundary = (L - 1) * oz

        def layer_of(l):
            return l * oz + (L - 1 - l) * gz

        loads_t = [
            pltpu.make_async_copy(
                tracers.at[:, layer_of(l)], t0.at[:, l + 1, pl.ds(8, N), :], sem_t.at[l]
            )
            for l in range(L)
        ]
        loads_w = [
            pltpu.make_async_copy(wind.at[:, layer_of(l)], wv.at[:, l], sem_w.at[l])
            for l in range(L)
        ]
        loads_f = [
            pltpu.make_async_copy(ref, floor.at[i], sem_f.at[i])
            for i, ref in enumerate((wall_in, exit_in, count_in))
        ]
        load_b = pltpu.make_async_copy(band_in, band, sem_b)
        for c in loads_t:
            c.start()
        for c in loads_f:
            c.start()
        for c in loads_w:
            c.start()
        load_b.start()

        barrier = pltpu.get_barrier_semaphore()

        def greet(*devs):
            for dev in devs:
                pl.semaphore_signal(barrier, inc=1, device_id=dev, device_id_type=MESH)

        greet((gx, gy, oz))
        pl.when(has_xn)(lambda: greet((gxn, gy, gz)))
        pl.when(has_xp)(lambda: greet((gxp, gy, gz), (gxp, gy, oz)))
        pl.when(has_yn)(lambda: greet((gx, gyn, gz)))
        pl.when(has_yp)(lambda: greet((gx, gyp, gz), (gx, gyp, oz)))
        pl.when(has_xp & has_yp)(lambda: greet((gxp, gyp, gz), (gxp, gyp, oz)))

        def clear(s, carry):
            t0[s, 0, pl.ds(8, N), :] = jnp.zeros((N, N), f32)
            t1[s, 0, pl.ds(8, N), :] = jnp.zeros((N, N), f32)
            return carry

        lax.fori_loop(0, SPECIES, clear, 0)

        def clear_rows(row):
            for s in range(SPECIES):
                for l in range(1, L + 1):
                    t0[s, l, pl.ds(row, 1), :] = jnp.zeros((1, N), f32)
                    t1[s, l, pl.ds(row, 1), :] = jnp.zeros((1, N), f32)

        er[:, :, pl.ds(0, 5), :] = jnp.zeros((2, SPECIES, 5, N), f32)
        m[:, :, pl.ds(0, 4), :] = jnp.zeros((3, 2, 4, N), f32)
        m[:, :, pl.ds(N + 12, 4), :] = jnp.zeros((3, 2, 4, N), f32)

        @pl.when(jnp.logical_not(has_xp))
        def _():
            clear_rows(7)
            er[:, :, pl.ds(5, 3), :] = jnp.zeros((2, SPECIES, 3, N), f32)
            m[:, :, pl.ds(4, 4), :] = jnp.zeros((3, 2, 4, N), f32)

        @pl.when(jnp.logical_not(has_xn))
        def _():
            clear_rows(N + 8)
            m[:, :, pl.ds(N + 8, 4), :] = jnp.zeros((3, 2, 4, N), f32)

        @pl.when(jnp.logical_not(has_yp))
        def _():
            for step in range(3):
                yr[step, 0] = jnp.zeros((72, N), f32)
            ec[0] = jnp.zeros((16, N), f32)
            ec[1] = jnp.zeros((16, N), f32)

        @pl.when(jnp.logical_not(has_yn))
        def _():
            for step in range(3):
                yr[step, 1] = jnp.zeros((72, N), f32)

        @pl.when(jnp.logical_not(has_xp & has_yp))
        def _():
            ec[2] = jnp.zeros((16, N), f32)
            ec[3] = jnp.zeros((16, N), f32)

        one = lambda flag: flag.astype(jnp.int32)
        pl.semaphore_wait(
            barrier,
            1 + 2 * one(has_xn) + one(has_xp) + 2 * one(has_yn) + one(has_yp)
            + 2 * one(has_xn) * one(has_yn),
        )

        def z_copy(step, s):
            src = tracers.at[s, boundary] if step == 0 else t1.at[s, L, pl.ds(8, N), :]
            dst = (t0 if step == 0 else t1).at[s, L + 1, pl.ds(8, N), :]
            return pltpu.make_async_remote_copy(
                src, dst, z_s.at[step, s], z_r.at[step, s],
                device_id=(gx, gy, oz), device_id_type=MESH,
            )

        def x_copies(step, d):
            dev = ((gxn if d == 0 else gxp), gy, gz)
            src, dst = ((N + 7, 7), (8, N + 8))[d]
            if step > 0:
                first, count = PARTS[step - 1]
                return [
                    pltpu.make_async_remote_copy(
                        t1.at[pl.ds(first, count), pl.ds(1, L), pl.ds(src, 1), :],
                        t1.at[pl.ds(first, count), pl.ds(1, L), pl.ds(dst, 1), :],
                        x_s.at[step, d, 0], x_r.at[step, d, 0],
                        device_id=dev, device_id_type=MESH,
                    )
                ]
            return [
                pltpu.make_async_remote_copy(
                    tracers.at[:, layer_of(l), pl.ds(src - 8, 1), :],
                    t0.at[:, l + 1, pl.ds(dst, 1), :],
                    x_s.at[0, d, l], x_r.at[0, d, l],
                    device_id=dev, device_id_type=MESH,
                )
                for l in range(L)
            ]

        def y_copy(step, d):
            first, rows = EDGE_ROWS[step]
            return pltpu.make_async_remote_copy(
                ys.at[step, pl.ds(first, rows), :], yr.at[step, d, pl.ds(first, rows), :],
                y_s.at[step, d], y_r.at[step, d],
                device_id=(gx, (gyn if d == 0 else gyp), gz), device_id_type=MESH,
            )

        def m_copy(d):
            src, dst = ((N + 4, 4), (8, N + 8))[d]
            return pltpu.make_async_remote_copy(
                m.at[:, :, pl.ds(src, 4), :], m.at[:, :, pl.ds(dst, 4), :],
                m_s.at[d], m_r.at[d],
                device_id=((gxn if d == 0 else gxp), gy, gz), device_id_type=MESH,
            )

        def send_x(step):
            for d in range(2):
                @pl.when(x_has[d])
                def _():
                    for c in x_copies(step, d):
                        c.start()

        def recv_x(step):
            for d in range(2):
                @pl.when(x_has[1 - d])
                def _():
                    for c in x_copies(step, d):
                        c.wait_recv()

        def recv_y(step):
            for d in range(2):
                pl.when(y_has[1 - d])(lambda: y_copy(step, d).wait_recv())

        def e_copy(s):
            return pltpu.make_async_remote_copy(
                e_own.at[s], e_oth.at[s], e_s.at[s], e_r.at[s],
                device_id=(gx, gy, oz), device_id_type=MESH,
            )

        def er_copy(s, d):
            return pltpu.make_async_remote_copy(
                e_own.at[s, pl.ds(N - 3, 3), :], er.at[d, s, pl.ds(5, 3), :],
                er_s.at[d, s], er_r.at[d, s],
                device_id=(gxn, gy, (gz if d == 0 else oz)), device_id_type=MESH,
            )

        def ec_copy(i):
            dev = ((gx, gyn, gz), (gx, gyn, oz), (gxn, gyn, gz), (gxn, gyn, oz))[i]
            return pltpu.make_async_remote_copy(
                es, ec.at[i], ec_s.at[i], ec_r.at[i], device_id=dev, device_id_type=MESH
            )

        send_x(0)
        z_copy(0, 0).start()
        z_copy(0, 1).start()

        lane = lax.broadcasted_iota(jnp.int32, (CHUNK, N), 1)
        chunks = tuple(range(0, N, CHUNK))

        def pack_y(src, s):
            for r in chunks:
                acc = ypack[pl.ds(r, CHUNK), :]
                for l in range(L):
                    j = 2 * (s * L + l)
                    c = src[s, l + 1, pl.ds(8 + r, CHUNK), :]
                    here = (lane == j + 1) | (lane == j + 2)
                    acc = jnp.where(here, pltpu.roll(c, j + 2, 1), acc)
                ypack[pl.ds(r, CHUNK), :] = acc

        def unpack_y(step):
            row = lax.broadcasted_iota(jnp.int32, (72, N), 0)
            before = yr[step, 0]
            after = yr[step, 1]
            after = jnp.where(row < 48, pltpu.roll(after, 70, 0), after)
            from_before = ((row < 48) & ((row & 1) == 1)) | ((row >= 48) & ((row & 7) < 4))
            both = jnp.where(from_before, before, after)
            yedge[...] = jnp.concatenate([both, jnp.zeros((N - 72, N), f32)], axis=0).T

        def send_y(step):
            ys[step] = ypack[...].T[:72]
            for d in range(2):
                pl.when(y_has[d])(lambda: y_copy(step, d).start())

        flip = (1 - 2 * gz).astype(f32)

        def moved(src, s, l, r, k):
            j = s * L + l
            c = src[s, l + 1, pl.ds(8 + r, CHUNK), :]
            total = c
            u = wv[0, l, pl.ds(r, CHUNK), :]
            total += (k + jnp.maximum(u, 0.0)) * (src[s, l + 1, pl.ds(7 + r, CHUNK), :] - c)
            total += (k - jnp.minimum(u, 0.0)) * (src[s, l + 1, pl.ds(9 + r, CHUNK), :] - c)
            u = wv[1, l, pl.ds(r, CHUNK), :]
            edge = pltpu.roll(yedge[pl.ds(r, CHUNK), :], N - 1 - 2 * j, 1)
            lower = jnp.where(lane == 0, edge, pltpu.roll(c, 1, 1))
            upper = jnp.where(lane == N - 1, edge, pltpu.roll(c, N - 1, 1))
            total += (k + jnp.maximum(u, 0.0)) * (lower - c)
            total += (k - jnp.minimum(u, 0.0)) * (upper - c)
            u = wv[2, l, pl.ds(r, CHUNK), :] * flip
            total += (k + jnp.maximum(u, 0.0)) * (src[s, l, pl.ds(8 + r, CHUNK), :] - c)
            total += (k - jnp.minimum(u, 0.0)) * (src[s, l + 2, pl.ds(8 + r, CHUNK), :] - c)
            return total

        for c in loads_f:
            c.wait()
        passable = 1.0 - floor[0].astype(f32)
        leave = 1.0 - 0.5 * floor[1].astype(f32)
        start = 0.25 * floor[2].astype(f32) * passable
        m[0, 0, pl.ds(8, N), :] = start
        m[1, 0, pl.ds(8, N), :] = passable
        m[2, 0, pl.ds(8, N), :] = leave
        wide = lax.broadcasted_iota(jnp.int32, (N, N), 1)
        acc = jnp.zeros((N, N), f32)
        for i, field in enumerate((start, passable, leave)):
            a = 48 + 8 * i
            acc = jnp.where((wide >= a) & (wide < a + 8), pltpu.roll(field, a + 4, 1), acc)
        ypack[...] = acc
        for c in loads_t:
            c.wait()

        def pack_y0(s, carry):
            pack_y(t0, s)
            return carry

        lax.fori_loop(0, SPECIES, pack_y0, 0)
        send_y(0)
        for s in range(2, SPECIES):
            z_copy(0, s).start()
        for c in loads_w:
            c.wait()
        load_b.wait()
        recv_y(0)
        unpack_y(0)

        for i in range(3):
            beside = pltpu.roll(yedge[...], N - 52 - 8 * i, 1)
            m[i, 1, pl.ds(8, N), :] = jnp.where((wide < 4) | (wide >= N - 4), beside, 0.0)
        for d in range(2):
            pl.when(x_has[d])(lambda: m_copy(d).start())
        recv_x(0)

        def first(s, carry):
            k = coefficient_of(s)
            z_copy(0, s).wait_recv()
            for l in (L - 1, 0, 1, 2):
                for r in chunks:
                    t1[s, l + 1, pl.ds(8 + r, CHUNK), :] = moved(t0, s, l, r, k)

            @pl.when(s != 2)
            def _():
                z_copy(1, s).start()

            pack_y(t1, s)
            return carry

        lax.fori_loop(0, 3, first, 0)
        send_x(1)
        send_y(1)
        z_copy(1, 2).start()
        lax.fori_loop(3, SPECIES, first, 0)
        send_x(2)
        send_y(2)

        for d in range(2):
            pl.when(x_has[1 - d])(lambda: m_copy(d).wait_recv())
        rows = N + 16
        lane_m = lax.broadcasted_iota(jnp.int32, (rows, N), 1)

        def y_lower(a, b):
            ra, rb = pltpu.roll(a, 1, 1), pltpu.roll(b, 1, 1)
            return jnp.where(lane_m == 0, rb, ra), jnp.where(lane_m == 0, ra, rb)

        def y_upper(a, b):
            ra, rb = pltpu.roll(a, N - 1, 1), pltpu.roll(b, N - 1, 1)
            return jnp.where(lane_m == N - 1, rb, ra), jnp.where(lane_m == N - 1, ra, rb)

        occ = [m[0, i] for i in range(2)]
        free = [m[1, i] for i in range(2)]
        out = [m[2, i] for i in range(2)]
        free_y = y_upper(*free)
        px = [0.25 * free[i] * pltpu.roll(free[i], rows - 1, 0) for i in range(2)]
        py = [0.15 * free[i] * free_y[i] for i in range(2)]
        for step in range(4):
            occ_yu = y_upper(*occ)
            occ_yl = y_lower(*occ)
            gate_x = [px[i] * (1.0 - pltpu.roll(occ[i], rows - 1, 0)) for i in range(2)]
            gate_y = [py[i] * (1.0 - occ_yu[i]) for i in range(2)]
            gate_yl = y_lower(*gate_y)
            after = []
            for i in range(2):
                stay = out[i] * (1.0 - gate_x[i] - gate_y[i])
                in_x = out[i] * pltpu.roll(gate_x[i], 1, 0)
                in_y = out[i] * gate_yl[i]
                c0[step, i] = stay[: N + 8]
                cx[step, i] = in_x[: N + 8]
                cy[step, i] = in_y[: N + 8]
                co[step, i] = (out[i] * occ[i])[: N + 8]
                after.append(stay * occ[i] + in_x * pltpu.roll(occ[i], 1, 0) + in_y * occ_yl[i])
            occ = after
        out_o[...] = occ[0][8 : N + 8]

        recv_x(1)
        recv_y(1)
        unpack_y(1)

        def in_band(l, r):
            b = band[pl.ds(r, CHUNK), :]
            layer = l * oz + (2 * L - 1 - l) * gz
            return (b == layer) | (b == layer - 1)

        def second(s, carry):
            k = coefficient_of(s)
            for r in chunks:
                acc = jnp.zeros((CHUNK, N), f32)
                for l in range(L - 1):
                    new = moved(t1, s, l, r, k)
                    out_t[s, layer_of(l), pl.ds(r, CHUNK), :] = new
                    acc += jnp.where(in_band(l, r), 0.5 * new, 0.0)
                e_own[s, pl.ds(r, CHUNK), :] = acc
            z_copy(1, s).wait_recv()
            for r in chunks:
                new = moved(t1, s, L - 1, r, k)
                out_t[s, boundary, pl.ds(r, CHUNK), :] = new
                e_own[s, pl.ds(r, CHUNK), :] += jnp.where(in_band(L - 1, r), 0.5 * new, 0.0)

            @pl.when(has_xn)
            def _():
                er_copy(s, 0).start()
                er_copy(s, 1).start()

            @pl.when(s < HOLD)
            def _():
                e_copy(s).start()

            return carry

        lax.fori_loop(0, 3, second, 0)
        recv_x(2)
        recv_y(2)
        unpack_y(2)
        lax.fori_loop(3, SPECIES, second, 0)
        strip = jnp.zeros((N, N), f32)
        for s in range(SPECIES):
            mine = (wide >= 3 * s) & (wide < 3 * s + 3)
            strip = jnp.where(mine, pltpu.roll(e_own[s], 3 * s + 3, 1), strip)
        es[...] = strip.T[:16]
        ec_to = (has_yn, has_yn, has_xn & has_yn, has_xn & has_yn)
        ec_from = (has_yp, has_yp, has_xp & has_yp, has_xp & has_yp)
        for i in range(4):
            pl.when(ec_to[i])(lambda: ec_copy(i).start())
        for s in range(HOLD, SPECIES):
            e_copy(s).start()

        def rate_of(co_, co2, hcn, o2, heat):
            return (
                0.3 * co_ * jnp.exp(0.3 * co2) + 0.2 * hcn
                + 0.1 * (2.0 - o2) * (2.0 - o2) + 0.1 * heat * heat
            )

        @pl.when(has_xp)
        def _():
            for s in range(SPECIES):
                er_copy(s, 0).wait_recv()
                er_copy(s, 1).wait_recv()

        edge = rate_of(*[er[0, s] + er[1, s] for s in range(SPECIES)])
        for i in range(4):
            pl.when(ec_from[i])(lambda: ec_copy(i).wait_recv())
        filler = jnp.zeros((N - 16, N), f32)
        side = jnp.concatenate([ec[0] + ec[1], filler], axis=0).T
        corner = jnp.concatenate([ec[2] + ec[3], filler], axis=0).T[N - 8 :]
        side = jnp.concatenate([corner, side], axis=0)
        side = rate_of(*[pltpu.roll(side, N - 3 - 3 * s, 1) for s in range(SPECIES)])
        for s in range(SPECIES):
            e_copy(s).wait_recv()
        middle = rate_of(*[e_own[s] + e_oth[s] for s in range(SPECIES)])
        lane_d = lax.broadcasted_iota(jnp.int32, (N + 8, N), 1)
        out_rate[0, pl.ds(0, 8), :] = edge
        out_rate[0, pl.ds(8, N), :] = middle
        out_rate[1] = jnp.where(lane_d >= N - 3, side, 0.0)

        for d in range(2):
            @pl.when(x_has[d])
            def _():
                for step in range(3):
                    for c in x_copies(step, d):
                        c.wait_send()
                m_copy(d).wait_send()

            @pl.when(y_has[d])
            def _():
                for step in range(3):
                    y_copy(step, d).wait_send()

        for s in range(SPECIES):
            z_copy(0, s).wait_send()
            z_copy(1, s).wait_send()
            e_copy(s).wait_send()

        @pl.when(has_xn)
        def _():
            for s in range(SPECIES):
                er_copy(s, 0).wait_send()
                er_copy(s, 1).wait_send()

        for i in range(4):
            pl.when(ec_to[i])(lambda: ec_copy(i).wait_send())

    return kernel


def finish(fields, occupants, c0, cx, cy, co, rate, out_t, out_o, out_f, dose_v, sem_t, sem_o, sem_f):
    copies = [
        pltpu.make_async_copy(fields.at[s], out_t.at[s], sem_t.at[s]) for s in range(SPECIES)
    ]
    copies.append(pltpu.make_async_copy(occupants, out_o, sem_o))
    for c in copies:
        c.start()
    lane = lax.broadcasted_iota(jnp.int32, (N + 8, N), 1)
    dose = [co[0, i] * rate[i] for i in range(2)]
    for step in range(1, 4):
        ra, rb = pltpu.roll(dose[0], 1, 1), pltpu.roll(dose[1], 1, 1)
        left = (jnp.where(lane == 0, rb, ra), jnp.where(lane == 0, ra, rb))
        dose = [
            c0[step, i] * dose[i] + cx[step, i] * pltpu.roll(dose[i], 1, 0)
            + cy[step, i] * left[i] + co[step, i] * rate[i]
            for i in range(2)
        ]
    dose_v[...] = dose[0][8:]
    copies.append(pltpu.make_async_copy(dose_v, out_f, sem_f))
    copies[-1].start()
    for c in copies:
        c.wait()


def solution(mesh):
    sizes = tuple(mesh.shape[name] for name in ("gx", "gy", "gz"))

    def on_device(tracers, wind_field, band_layer, wall_mask, exit_mask, occupant_count):
        floor = jax.ShapeDtypeStruct((N, N), f32)
        hbm = pl.BlockSpec(memory_space=pltpu.HBM)
        vmem = pl.BlockSpec(memory_space=pltpu.VMEM)
        V = pltpu.VMEM
        D = pltpu.SemaphoreType.DMA
        weights = jax.ShapeDtypeStruct((4, 2, N + 8, N), f32)
        cells = jax.ShapeDtypeStruct((SPECIES, L, N, N), f32)
        found = pl.pallas_call(
            make_kernel(sizes),
            out_shape=(
                cells, floor, weights, weights, weights, weights,
                jax.ShapeDtypeStruct((2, N + 8, N), f32),
            ),
            in_specs=[hbm] * 6,
            out_specs=(vmem,) * 7,
            scratch_shapes=[
                V((SPECIES, L + 2, N + 16, N), f32),
                V((SPECIES, L + 2, N + 16, N), f32),
                V((3, L, N, N), f32),
                V((N, N), jnp.int32),
                V((3, N, N), jnp.int32),
                V((N, N), f32), V((N, N), f32),
                V((3, 72, N), f32), V((3, 2, 72, N), f32),
                V((3, 2, N + 16, N), f32),
                V((SPECIES, N, N), f32), V((SPECIES, N, N), f32),
                V((2, SPECIES, 8, N), f32),
                V((16, N), f32), V((4, 16, N), f32),
                D((L,)), D((L,)), D, D((3,)),
                D((2, SPECIES)), D((2, SPECIES)),
                D((3, 2, L)), D((3, 2, L)), D((3, 2)), D((3, 2)), D((2,)), D((2,)),
                D((SPECIES,)), D((SPECIES,)), D((2, SPECIES)), D((2, SPECIES)),
                D((4,)), D((4,)),
            ],
            compiler_params=pltpu.CompilerParams(
                collective_id=0, has_side_effects=True, vmem_limit_bytes=32 * 1024 * 1024
            ),
        )(*[pltpu.with_memory_space_constraint(a, pltpu.HBM) for a in (tracers, wind_field, band_layer, wall_mask, exit_mask, occupant_count)])
        return pl.pallas_call(
            finish,
            out_shape=(cells, floor, floor),
            in_specs=[vmem] * 7,
            out_specs=(hbm,) * 3,
            scratch_shapes=[V((N, N), f32), D((SPECIES,)), D, D],
            compiler_params=pltpu.CompilerParams(vmem_limit_bytes=16 * 1024 * 1024),
        )(*found)

    return jax.shard_map(
        on_device,
        mesh=mesh,
        in_specs=(
            P(None, "gz", "gx", "gy"),
            P(None, "gz", "gx", "gy"),
            P("gx", "gy"),
            P("gx", "gy"),
            P("gx", "gy"),
            P("gx", "gy"),
        ),
        out_specs=(P(None, "gz", "gx", "gy"), P("gx", "gy"), P("gx", "gy")),
        check_vma=False,
    )
```

```python
import jax
import jax.numpy as jnp
from jax import lax
from jax.experimental import pallas as pl
from jax.experimental.pallas import tpu as pltpu
from jax.sharding import PartitionSpec as P

diffusivity = (0.05, 0.04, 0.06, 0.03, 0.045)
SPECIES = 5
L = 4
N = 128
CHUNK = 32
HOLD = 3
BEFORE = 4
PARTS = ((0, 3), (3, 2))
EDGE_ROWS = ((0, 72), (0, 32), (24, 24))
MESH = pl.DeviceIdType.MESH
f32 = jnp.float32


def coefficient_of(s):
    k = jnp.float32(diffusivity[0])
    for i in range(1, SPECIES):
        k = jnp.where(s == i, jnp.float32(diffusivity[i]), k)
    return k


def make_kernel(sizes):
    nx, ny, nz = sizes

    def kernel(
        tracers, wind, band_in, wall_in, exit_in, count_in,
        out_t, out_o, c0, cx, cy, co, out_rate,
        t0, t1, wv, band, floor,
        yedge, ypack, ys, yr,
        m,
        e_own, e_oth, er, es, ec,
        sem_t, sem_w, sem_b, sem_f,
        z_s, z_r, x_s, x_r, y_s, y_r, m_s, m_r,
        e_s, e_r, er_s, er_r, ec_s, ec_r, here_x, here_y,
    ):
        gx, gy, gz = lax.axis_index("gx"), lax.axis_index("gy"), lax.axis_index("gz")
        oz = 1 - gz
        gxn, gxp, gyn, gyp = gx + 1, gx - 1, gy + 1, gy - 1
        has_xn, has_xp, has_yn, has_yp = gx < nx - 1, gx > 0, gy < ny - 1, gy > 0
        x_has = (has_xn, has_xp)
        y_has = (has_yn, has_yp)
        boundary = (L - 1) * oz

        def layer_of(l):
            return l * oz + (L - 1 - l) * gz

        loads_t = [
            pltpu.make_async_copy(
                tracers.at[:, layer_of(l)], t0.at[:, l + 1, pl.ds(8, N), :], sem_t.at[l]
            )
            for l in range(L)
        ]
        loads_w = [
            pltpu.make_async_copy(wind.at[:, layer_of(l)], wv.at[:, l], sem_w.at[l])
            for l in range(L)
        ]
        loads_f = [
            pltpu.make_async_copy(ref, floor.at[i], sem_f.at[i])
            for i, ref in enumerate((wall_in, exit_in, count_in))
        ]
        load_b = pltpu.make_async_copy(band_in, band, sem_b)
        for c in loads_t:
            c.start()
        for c in loads_f:
            c.start()
        for c in loads_w:
            c.start()
        load_b.start()

        barrier = pltpu.get_barrier_semaphore()

        def greet(*devs):
            for dev in devs:
                pl.semaphore_signal(barrier, inc=1, device_id=dev, device_id_type=MESH)

        greet((gx, gy, oz))
        odd_y, even_y = lax.rem(gy, 2) == 1, lax.rem(gy, 2) == 0
        speaks_x = ((gx > 0) & has_xn, gx == 1)
        waits_x = ((gx == 0) & has_xn, gx > 1)
        x_dev = ((gxn, gy, gz), (gxp, gy, gz))
        y_dev = ((gx, gyn, gz), (gx, gyp, gz))
        for d in range(2):
            pl.when(speaks_x[d])(lambda: greet(x_dev[d]))
            pl.when(odd_y & y_has[d])(lambda: greet(y_dev[d]))

        def clear(s, carry):
            t0[s, 0, pl.ds(8, N), :] = jnp.zeros((N, N), f32)
            t1[s, 0, pl.ds(8, N), :] = jnp.zeros((N, N), f32)
            return carry

        lax.fori_loop(0, SPECIES, clear, 0)

        def clear_rows(row):
            for s in range(SPECIES):
                for l in range(1, L + 1):
                    t0[s, l, pl.ds(row, 1), :] = jnp.zeros((1, N), f32)
                    t1[s, l, pl.ds(row, 1), :] = jnp.zeros((1, N), f32)

        er[:, :, pl.ds(0, 5), :] = jnp.zeros((2, SPECIES, 5, N), f32)
        m[:, :, pl.ds(0, 4), :] = jnp.zeros((3, 2, 4, N), f32)
        m[:, :, pl.ds(N + 12, 4), :] = jnp.zeros((3, 2, 4, N), f32)

        @pl.when(jnp.logical_not(has_xp))
        def _():
            clear_rows(7)
            er[:, :, pl.ds(5, 3), :] = jnp.zeros((2, SPECIES, 3, N), f32)
            m[:, :, pl.ds(4, 4), :] = jnp.zeros((3, 2, 4, N), f32)

        @pl.when(jnp.logical_not(has_xn))
        def _():
            clear_rows(N + 8)
            m[:, :, pl.ds(N + 8, 4), :] = jnp.zeros((3, 2, 4, N), f32)

        @pl.when(jnp.logical_not(has_yp))
        def _():
            for step in range(3):
                yr[step, 0] = jnp.zeros((72, N), f32)
            ec[0] = jnp.zeros((16, N), f32)
            ec[1] = jnp.zeros((16, N), f32)

        @pl.when(jnp.logical_not(has_yn))
        def _():
            for step in range(3):
                yr[step, 1] = jnp.zeros((72, N), f32)

        @pl.when(jnp.logical_not(has_xp & has_yp))
        def _():
            ec[2] = jnp.zeros((16, N), f32)
            ec[3] = jnp.zeros((16, N), f32)

        one = lambda flag: flag.astype(jnp.int32)
        pl.semaphore_wait(
            barrier,
            1 + one(waits_x[0]) + one(waits_x[1])
            + one(even_y) * (one(has_yn) + one(has_yp)),
        )

        def answer(sem, dev):
            pl.semaphore_signal(sem, inc=1, device_id=dev, device_id_type=MESH)

        for d in range(2):
            pl.when(waits_x[d])(lambda: answer(here_x.at[1 - d], x_dev[d]))
            pl.when(even_y & y_has[d])(lambda: answer(here_y.at[1 - d], y_dev[d]))

        def z_copy(step, s):
            src = tracers.at[s, boundary] if step == 0 else t1.at[s, L, pl.ds(8, N), :]
            dst = (t0 if step == 0 else t1).at[s, L + 1, pl.ds(8, N), :]
            return pltpu.make_async_remote_copy(
                src, dst, z_s.at[step, s], z_r.at[step, s],
                device_id=(gx, gy, oz), device_id_type=MESH,
            )

        def x_copies(step, d):
            dev = ((gxn if d == 0 else gxp), gy, gz)
            src, dst = ((N + 7, 7), (8, N + 8))[d]
            if step > 0:
                first, count = PARTS[step - 1]
                return [
                    pltpu.make_async_remote_copy(
                        t1.at[pl.ds(first, count), pl.ds(1, L), pl.ds(src, 1), :],
                        t1.at[pl.ds(first, count), pl.ds(1, L), pl.ds(dst, 1), :],
                        x_s.at[step, d, 0], x_r.at[step, d, 0],
                        device_id=dev, device_id_type=MESH,
                    )
                ]
            return [
                pltpu.make_async_remote_copy(
                    tracers.at[:, layer_of(l), pl.ds(src - 8, 1), :],
                    t0.at[:, l + 1, pl.ds(dst, 1), :],
                    x_s.at[0, d, l], x_r.at[0, d, l],
                    device_id=dev, device_id_type=MESH,
                )
                for l in range(L)
            ]

        def y_copy(step, d):
            first, rows = EDGE_ROWS[step]
            return pltpu.make_async_remote_copy(
                ys.at[step, pl.ds(first, rows), :], yr.at[step, d, pl.ds(first, rows), :],
                y_s.at[step, d], y_r.at[step, d],
                device_id=(gx, (gyn if d == 0 else gyp), gz), device_id_type=MESH,
            )

        def m_copy(d):
            src, dst = ((N + 4, 4), (8, N + 8))[d]
            return pltpu.make_async_remote_copy(
                m.at[:, :, pl.ds(src, 4), :], m.at[:, :, pl.ds(dst, 4), :],
                m_s.at[d], m_r.at[d],
                device_id=((gxn if d == 0 else gxp), gy, gz), device_id_type=MESH,
            )

        def send_x(step, when=x_has):
            for d in range(2):
                @pl.when(when[d])
                def _():
                    for c in x_copies(step, d):
                        c.start()

        def recv_x(step):
            for d in range(2):
                @pl.when(x_has[1 - d])
                def _():
                    for c in x_copies(step, d):
                        c.wait_recv()

        def recv_y(step):
            for d in range(2):
                pl.when(y_has[1 - d])(lambda: y_copy(step, d).wait_recv())

        def e_copy(s):
            return pltpu.make_async_remote_copy(
                e_own.at[s], e_oth.at[s], e_s.at[s], e_r.at[s],
                device_id=(gx, gy, oz), device_id_type=MESH,
            )

        def er_copy(s, d):
            return pltpu.make_async_remote_copy(
                e_own.at[s, pl.ds(N - 3, 3), :], er.at[d, s, pl.ds(5, 3), :],
                er_s.at[d, s], er_r.at[d, s],
                device_id=(gxn, gy, (gz if d == 0 else oz)), device_id_type=MESH,
            )

        def ec_copy(i):
            dev = ((gx, gyn, gz), (gx, gyn, oz), (gxn, gyn, gz), (gx, gy, oz))[i]
            return pltpu.make_async_remote_copy(
                (ec.at[2] if i == 3 else es), ec.at[i], ec_s.at[i], ec_r.at[i],
                device_id=dev, device_id_type=MESH,
            )

        send_x(0, waits_x)
        z_copy(0, 0).start()
        z_copy(0, 1).start()

        lane = lax.broadcasted_iota(jnp.int32, (CHUNK, N), 1)
        chunks = tuple(range(0, N, CHUNK))

        def pack_y(src, s):
            for r in chunks:
                acc = ypack[pl.ds(r, CHUNK), :]
                for l in range(L):
                    j = 2 * (s * L + l)
                    c = src[s, l + 1, pl.ds(8 + r, CHUNK), :]
                    here = (lane == j + 1) | (lane == j + 2)
                    acc = jnp.where(here, pltpu.roll(c, j + 2, 1), acc)
                ypack[pl.ds(r, CHUNK), :] = acc

        def unpack_y(step):
            row = lax.broadcasted_iota(jnp.int32, (72, N), 0)
            before = yr[step, 0]
            after = yr[step, 1]
            after = jnp.where(row < 48, pltpu.roll(after, 70, 0), after)
            from_before = ((row < 48) & ((row & 1) == 1)) | ((row >= 48) & ((row & 7) < 4))
            both = jnp.where(from_before, before, after)
            yedge[...] = jnp.concatenate([both, jnp.zeros((N - 72, N), f32)], axis=0).T

        def send_y(step):
            ys[step] = ypack[...].T[:72]
            for d in range(2):
                pl.when(y_has[d])(lambda: y_copy(step, d).start())

        flip = (1 - 2 * gz).astype(f32)

        def moved(src, s, l, r, k):
            j = s * L + l
            c = src[s, l + 1, pl.ds(8 + r, CHUNK), :]
            total = c
            u = wv[0, l, pl.ds(r, CHUNK), :]
            total += (k + jnp.maximum(u, 0.0)) * (src[s, l + 1, pl.ds(7 + r, CHUNK), :] - c)
            total += (k - jnp.minimum(u, 0.0)) * (src[s, l + 1, pl.ds(9 + r, CHUNK), :] - c)
            u = wv[1, l, pl.ds(r, CHUNK), :]
            edge = pltpu.roll(yedge[pl.ds(r, CHUNK), :], N - 1 - 2 * j, 1)
            lower = jnp.where(lane == 0, edge, pltpu.roll(c, 1, 1))
            upper = jnp.where(lane == N - 1, edge, pltpu.roll(c, N - 1, 1))
            total += (k + jnp.maximum(u, 0.0)) * (lower - c)
            total += (k - jnp.minimum(u, 0.0)) * (upper - c)
            u = wv[2, l, pl.ds(r, CHUNK), :] * flip
            total += (k + jnp.maximum(u, 0.0)) * (src[s, l, pl.ds(8 + r, CHUNK), :] - c)
            total += (k - jnp.minimum(u, 0.0)) * (src[s, l + 2, pl.ds(8 + r, CHUNK), :] - c)
            return total

        for c in loads_f:
            c.wait()
        passable = 1.0 - floor[0].astype(f32)
        leave = 1.0 - 0.5 * floor[1].astype(f32)
        start = 0.25 * floor[2].astype(f32) * passable
        m[0, 0, pl.ds(8, N), :] = start
        m[1, 0, pl.ds(8, N), :] = passable
        m[2, 0, pl.ds(8, N), :] = leave
        wide = lax.broadcasted_iota(jnp.int32, (N, N), 1)
        acc = jnp.zeros((N, N), f32)
        for i, field in enumerate((start, passable, leave)):
            a = 48 + 8 * i
            acc = jnp.where((wide >= a) & (wide < a + 8), pltpu.roll(field, a + 4, 1), acc)
        ypack[...] = acc
        for c in loads_t:
            c.wait()

        def pack_y0(s, carry):
            pack_y(t0, s)
            return carry

        lax.fori_loop(0, SPECIES, pack_y0, 0)
        for s in range(2, BEFORE):
            z_copy(0, s).start()

        for d in range(2):
            pl.when(speaks_x[d])(lambda: pl.semaphore_wait(here_x.at[d], 1))
        send_x(0, speaks_x)
        for d in range(2):
            pl.when(odd_y & y_has[d])(lambda: pl.semaphore_wait(here_y.at[d], 1))
        send_y(0)
        for s in range(BEFORE, SPECIES):
            z_copy(0, s).start()
        for c in loads_w:
            c.wait()
        load_b.wait()
        recv_y(0)
        unpack_y(0)

        for i in range(3):
            beside = pltpu.roll(yedge[...], N - 52 - 8 * i, 1)
            m[i, 1, pl.ds(8, N), :] = jnp.where((wide < 4) | (wide >= N - 4), beside, 0.0)
        for d in range(2):
            pl.when(x_has[d])(lambda: m_copy(d).start())
        recv_x(0)

        def first(s, carry):
            k = coefficient_of(s)
            z_copy(0, s).wait_recv()
            for l in (L - 1, 0, 1, 2):
                for r in chunks:
                    t1[s, l + 1, pl.ds(8 + r, CHUNK), :] = moved(t0, s, l, r, k)

            @pl.when(s != 2)
            def _():
                z_copy(1, s).start()

            pack_y(t1, s)
            return carry

        lax.fori_loop(0, 3, first, 0)
        send_x(1)
        send_y(1)
        z_copy(1, 2).start()
        lax.fori_loop(3, SPECIES, first, 0)
        send_x(2)
        send_y(2)

        for d in range(2):
            pl.when(x_has[1 - d])(lambda: m_copy(d).wait_recv())
        rows = N + 16
        lane_m = lax.broadcasted_iota(jnp.int32, (rows, N), 1)

        def y_lower(a, b):
            ra, rb = pltpu.roll(a, 1, 1), pltpu.roll(b, 1, 1)
            return jnp.where(lane_m == 0, rb, ra), jnp.where(lane_m == 0, ra, rb)

        def y_upper(a, b):
            ra, rb = pltpu.roll(a, N - 1, 1), pltpu.roll(b, N - 1, 1)
            return jnp.where(lane_m == N - 1, rb, ra), jnp.where(lane_m == N - 1, ra, rb)

        occ = [m[0, i] for i in range(2)]
        free = [m[1, i] for i in range(2)]
        out = [m[2, i] for i in range(2)]
        free_y = y_upper(*free)
        px = [0.25 * free[i] * pltpu.roll(free[i], rows - 1, 0) for i in range(2)]
        py = [0.15 * free[i] * free_y[i] for i in range(2)]
        for step in range(4):
            occ_yu = y_upper(*occ)
            occ_yl = y_lower(*occ)
            gate_x = [px[i] * (1.0 - pltpu.roll(occ[i], rows - 1, 0)) for i in range(2)]
            gate_y = [py[i] * (1.0 - occ_yu[i]) for i in range(2)]
            gate_yl = y_lower(*gate_y)
            after = []
            for i in range(2):
                stay = out[i] * (1.0 - gate_x[i] - gate_y[i])
                in_x = out[i] * pltpu.roll(gate_x[i], 1, 0)
                in_y = out[i] * gate_yl[i]
                c0[step, i] = stay[: N + 8]
                cx[step, i] = in_x[: N + 8]
                cy[step, i] = in_y[: N + 8]
                co[step, i] = (out[i] * occ[i])[: N + 8]
                after.append(stay * occ[i] + in_x * pltpu.roll(occ[i], 1, 0) + in_y * occ_yl[i])
            occ = after
        out_o[...] = occ[0][8 : N + 8]

        recv_x(1)
        recv_y(1)
        unpack_y(1)

        def in_band(l, r):
            b = band[pl.ds(r, CHUNK), :]
            layer = l * oz + (2 * L - 1 - l) * gz
            return (b == layer) | (b == layer - 1)

        def second(s, carry):
            k = coefficient_of(s)
            for r in chunks:
                acc = jnp.zeros((CHUNK, N), f32)
                for l in range(L - 1):
                    new = moved(t1, s, l, r, k)
                    out_t[s, layer_of(l), pl.ds(r, CHUNK), :] = new
                    acc += jnp.where(in_band(l, r), 0.5 * new, 0.0)
                e_own[s, pl.ds(r, CHUNK), :] = acc
            z_copy(1, s).wait_recv()
            for r in chunks:
                new = moved(t1, s, L - 1, r, k)
                out_t[s, boundary, pl.ds(r, CHUNK), :] = new
                e_own[s, pl.ds(r, CHUNK), :] += jnp.where(in_band(L - 1, r), 0.5 * new, 0.0)

            @pl.when(has_xn)
            def _():
                er_copy(s, 0).start()
                er_copy(s, 1).start()

            @pl.when(s < HOLD)
            def _():
                e_copy(s).start()

            return carry

        lax.fori_loop(0, 3, second, 0)
        recv_x(2)
        recv_y(2)
        unpack_y(2)
        lax.fori_loop(3, SPECIES, second, 0)
        strip = jnp.zeros((N, N), f32)
        for s in range(SPECIES):
            mine = (wide >= 3 * s) & (wide < 3 * s + 3)
            strip = jnp.where(mine, pltpu.roll(e_own[s], 3 * s + 3, 1), strip)
        es[...] = strip.T[:16]
        ec_to = (has_yn, has_yn, has_xn & has_yn, has_xp & has_yp)
        ec_from = (has_yp, has_yp, has_xp & has_yp, has_xp & has_yp)
        for i in range(3):
            pl.when(ec_to[i])(lambda: ec_copy(i).start())
        for s in range(HOLD, SPECIES):
            e_copy(s).start()

        def rate_of(co_, co2, hcn, o2, heat):
            return (
                0.3 * co_ * jnp.exp(0.3 * co2) + 0.2 * hcn
                + 0.1 * (2.0 - o2) * (2.0 - o2) + 0.1 * heat * heat
            )

        @pl.when(has_xp)
        def _():
            for s in range(SPECIES):
                er_copy(s, 0).wait_recv()
                er_copy(s, 1).wait_recv()

        edge = rate_of(*[er[0, s] + er[1, s] for s in range(SPECIES)])
        for i in range(3):
            pl.when(ec_from[i])(lambda: ec_copy(i).wait_recv())
        pl.when(ec_from[3])(lambda: ec_copy(3).start())
        pl.when(ec_from[3])(lambda: ec_copy(3).wait_recv())
        filler = jnp.zeros((N - 16, N), f32)
        side = jnp.concatenate([ec[0] + ec[1], filler], axis=0).T
        corner = jnp.concatenate([ec[2] + ec[3], filler], axis=0).T[N - 8 :]
        side = jnp.concatenate([corner, side], axis=0)
        side = rate_of(*[pltpu.roll(side, N - 3 - 3 * s, 1) for s in range(SPECIES)])
        for s in range(SPECIES):
            e_copy(s).wait_recv()
        middle = rate_of(*[e_own[s] + e_oth[s] for s in range(SPECIES)])
        lane_d = lax.broadcasted_iota(jnp.int32, (N + 8, N), 1)
        out_rate[0, pl.ds(0, 8), :] = edge
        out_rate[0, pl.ds(8, N), :] = middle
        out_rate[1] = jnp.where(lane_d >= N - 3, side, 0.0)

        for d in range(2):
            @pl.when(x_has[d])
            def _():
                for step in range(3):
                    for c in x_copies(step, d):
                        c.wait_send()
                m_copy(d).wait_send()

            @pl.when(y_has[d])
            def _():
                for step in range(3):
                    y_copy(step, d).wait_send()

        for s in range(SPECIES):
            z_copy(0, s).wait_send()
            z_copy(1, s).wait_send()
            e_copy(s).wait_send()

        @pl.when(has_xn)
        def _():
            for s in range(SPECIES):
                er_copy(s, 0).wait_send()
                er_copy(s, 1).wait_send()

        for i in range(4):
            pl.when(ec_to[i])(lambda: ec_copy(i).wait_send())

    return kernel


def finish(fields, occupants, c0, cx, cy, co, rate, out_t, out_o, out_f, dose_v, sem_t, sem_o, sem_f):
    copies = [
        pltpu.make_async_copy(fields.at[s], out_t.at[s], sem_t.at[s]) for s in range(SPECIES)
    ]
    copies.append(pltpu.make_async_copy(occupants, out_o, sem_o))
    for c in copies:
        c.start()
    lane = lax.broadcasted_iota(jnp.int32, (N + 8, N), 1)
    dose = [co[0, i] * rate[i] for i in range(2)]
    for step in range(1, 4):
        ra, rb = pltpu.roll(dose[0], 1, 1), pltpu.roll(dose[1], 1, 1)
        left = (jnp.where(lane == 0, rb, ra), jnp.where(lane == 0, ra, rb))
        dose = [
            c0[step, i] * dose[i] + cx[step, i] * pltpu.roll(dose[i], 1, 0)
            + cy[step, i] * left[i] + co[step, i] * rate[i]
            for i in range(2)
        ]
    dose_v[...] = dose[0][8:]
    copies.append(pltpu.make_async_copy(dose_v, out_f, sem_f))
    copies[-1].start()
    for c in copies:
        c.wait()


def solution(mesh):
    sizes = tuple(mesh.shape[name] for name in ("gx", "gy", "gz"))

    def on_device(tracers, wind_field, band_layer, wall_mask, exit_mask, occupant_count):
        floor = jax.ShapeDtypeStruct((N, N), f32)
        hbm = pl.BlockSpec(memory_space=pltpu.HBM)
        vmem = pl.BlockSpec(memory_space=pltpu.VMEM)
        V = pltpu.VMEM
        D = pltpu.SemaphoreType.DMA
        R = pltpu.SemaphoreType.REGULAR
        weights = jax.ShapeDtypeStruct((4, 2, N + 8, N), f32)
        cells = jax.ShapeDtypeStruct((SPECIES, L, N, N), f32)
        found = pl.pallas_call(
            make_kernel(sizes),
            out_shape=(
                cells, floor, weights, weights, weights, weights,
                jax.ShapeDtypeStruct((2, N + 8, N), f32),
            ),
            in_specs=[hbm] * 6,
            out_specs=(vmem,) * 7,
            scratch_shapes=[
                V((SPECIES, L + 2, N + 16, N), f32),
                V((SPECIES, L + 2, N + 16, N), f32),
                V((3, L, N, N), f32),
                V((N, N), jnp.int32),
                V((3, N, N), jnp.int32),
                V((N, N), f32), V((N, N), f32),
                V((3, 72, N), f32), V((3, 2, 72, N), f32),
                V((3, 2, N + 16, N), f32),
                V((SPECIES, N, N), f32), V((SPECIES, N, N), f32),
                V((2, SPECIES, 8, N), f32),
                V((16, N), f32), V((4, 16, N), f32),
                D((L,)), D((L,)), D, D((3,)),
                D((2, SPECIES)), D((2, SPECIES)),
                D((3, 2, L)), D((3, 2, L)), D((3, 2)), D((3, 2)), D((2,)), D((2,)),
                D((SPECIES,)), D((SPECIES,)), D((2, SPECIES)), D((2, SPECIES)),
                D((4,)), D((4,)),
                R((2,)), R((2,)),
            ],
            compiler_params=pltpu.CompilerParams(
                collective_id=0, has_side_effects=True, vmem_limit_bytes=32 * 1024 * 1024
            ),
        )(*[pltpu.with_memory_space_constraint(a, pltpu.HBM) for a in (tracers, wind_field, band_layer, wall_mask, exit_mask, occupant_count)])
        return pl.pallas_call(
            finish,
            out_shape=(cells, floor, floor),
            in_specs=[vmem] * 7,
            out_specs=(hbm,) * 3,
            scratch_shapes=[V((N, N), f32), D((SPECIES,)), D, D],
            compiler_params=pltpu.CompilerParams(vmem_limit_bytes=16 * 1024 * 1024),
        )(*found)

    return jax.shard_map(
        on_device,
        mesh=mesh,
        in_specs=(
            P(None, "gz", "gx", "gy"),
            P(None, "gz", "gx", "gy"),
            P("gx", "gy"),
            P("gx", "gy"),
            P("gx", "gy"),
            P("gx", "gy"),
        ),
        out_specs=(P(None, "gz", "gx", "gy"), P("gx", "gy"), P("gx", "gy")),
        check_vma=False,
    )
```

```python
import functools

import jax
import jax.numpy as jnp
from jax import lax
from jax.experimental import pallas as pl
from jax.experimental.pallas import tpu as pltpu
from jax.sharding import PartitionSpec as P

diffusivity = (0.05, 0.04, 0.06, 0.03, 0.045)
SPECIES = 5
L = 4
N = 128
CHUNK = 32
HOLD = 3
BEFORE = 4
PARTS = ((0, 3), (3, 2))
EDGE_ROWS = ((0, 72), (0, 32), (24, 24))
MESH = pl.DeviceIdType.MESH
f32 = jnp.float32


def coefficient_of(s):
    k = jnp.float32(diffusivity[0])
    for i in range(1, SPECIES):
        k = jnp.where(s == i, jnp.float32(diffusivity[i]), k)
    return k


def make_kernel(sizes):
    nx, ny, nz = sizes

    def kernel(
        tracers, wind, band_in, wall_in, exit_in, count_in,
        out_t, out_o, c0, cx, cy, co, out_rate,
        t0, t1, wv, band, floor,
        yedge, ypack, ys, yr, xs, xr,
        m,
        e_own, e_oth, er, es, ec,
        sem_t, sem_w, sem_b, sem_f,
        z_s, z_r, x_s, x_r, y_s, y_r, m_s, m_r,
        e_s, e_r, er_s, er_r, ec_s, ec_r, here_x, here_y,
    ):
        gx, gy, gz = lax.axis_index("gx"), lax.axis_index("gy"), lax.axis_index("gz")
        oz = 1 - gz
        gxn, gxp, gyn, gyp = gx + 1, gx - 1, gy + 1, gy - 1
        has_xn, has_xp, has_yn, has_yp = gx < nx - 1, gx > 0, gy < ny - 1, gy > 0
        x_has = (has_xn, has_xp)
        y_has = (has_yn, has_yp)
        boundary = (L - 1) * oz

        def layer_of(l):
            return l * oz + (L - 1 - l) * gz

        loads_t = [
            pltpu.make_async_copy(
                tracers.at[:, layer_of(l)], t0.at[:, l + 1, pl.ds(8, N), :], sem_t.at[l]
            )
            for l in range(L)
        ]
        loads_w = [
            pltpu.make_async_copy(wind.at[:, layer_of(l)], wv.at[:, l], sem_w.at[l])
            for l in range(L)
        ]
        loads_f = [
            pltpu.make_async_copy(ref, floor.at[i], sem_f.at[i])
            for i, ref in enumerate((wall_in, exit_in, count_in))
        ]
        load_b = pltpu.make_async_copy(band_in, band, sem_b)
        for c in loads_t:
            c.start()
        for c in loads_f:
            c.start()
        for c in loads_w:
            c.start()
        load_b.start()

        barrier = pltpu.get_barrier_semaphore()

        def greet(*devs):
            for dev in devs:
                pl.semaphore_signal(barrier, inc=1, device_id=dev, device_id_type=MESH)

        greet((gx, gy, oz))
        odd_y, even_y = lax.rem(gy, 2) == 1, lax.rem(gy, 2) == 0
        speaks_x = ((gx > 0) & has_xn, gx == 1)
        waits_x = ((gx == 0) & has_xn, gx > 1)
        x_dev = ((gxn, gy, gz), (gxp, gy, gz))
        y_dev = ((gx, gyn, gz), (gx, gyp, gz))
        for d in range(2):
            pl.when(speaks_x[d])(lambda: greet(x_dev[d]))
            pl.when(odd_y & y_has[d])(lambda: greet(y_dev[d]))

        def clear(s, carry):
            t0[s, 0, pl.ds(8, N), :] = jnp.zeros((N, N), f32)
            t1[s, 0, pl.ds(8, N), :] = jnp.zeros((N, N), f32)
            return carry

        lax.fori_loop(0, SPECIES, clear, 0)

        def clear_rows(row):
            for s in range(SPECIES):
                for l in range(1, L + 1):
                    t0[s, l, pl.ds(row, 1), :] = jnp.zeros((1, N), f32)
                    t1[s, l, pl.ds(row, 1), :] = jnp.zeros((1, N), f32)

        er[:, :, pl.ds(0, 5), :] = jnp.zeros((2, SPECIES, 5, N), f32)
        m[:, :, pl.ds(0, 4), :] = jnp.zeros((3, 2, 4, N), f32)
        m[:, :, pl.ds(N + 12, 4), :] = jnp.zeros((3, 2, 4, N), f32)

        @pl.when(jnp.logical_not(has_xp))
        def _():
            clear_rows(7)
            er[:, :, pl.ds(5, 3), :] = jnp.zeros((2, SPECIES, 3, N), f32)
            m[:, :, pl.ds(4, 4), :] = jnp.zeros((3, 2, 4, N), f32)

        @pl.when(jnp.logical_not(has_xn))
        def _():
            clear_rows(N + 8)
            m[:, :, pl.ds(N + 8, 4), :] = jnp.zeros((3, 2, 4, N), f32)

        @pl.when(jnp.logical_not(has_yp))
        def _():
            for step in range(3):
                yr[step, 0] = jnp.zeros((72, N), f32)
            ec[0] = jnp.zeros((16, N), f32)
            ec[1] = jnp.zeros((16, N), f32)

        @pl.when(jnp.logical_not(has_yn))
        def _():
            for step in range(3):
                yr[step, 1] = jnp.zeros((72, N), f32)

        @pl.when(jnp.logical_not(has_xp & has_yp))
        def _():
            ec[2] = jnp.zeros((16, N), f32)
            ec[3] = jnp.zeros((16, N), f32)

        one = lambda flag: flag.astype(jnp.int32)
        pl.semaphore_wait(
            barrier,
            1 + one(waits_x[0]) + one(waits_x[1])
            + one(even_y) * (one(has_yn) + one(has_yp)),
        )

        def answer(sem, dev):
            pl.semaphore_signal(sem, inc=1, device_id=dev, device_id_type=MESH)

        for d in range(2):
            pl.when(waits_x[d])(lambda: answer(here_x.at[1 - d], x_dev[d]))
            pl.when(even_y & y_has[d])(lambda: answer(here_y.at[1 - d], y_dev[d]))

        def z_copy(step, s):
            src = tracers.at[s, boundary] if step == 0 else t1.at[s, L, pl.ds(8, N), :]
            dst = (t0 if step == 0 else t1).at[s, L + 1, pl.ds(8, N), :]
            return pltpu.make_async_remote_copy(
                src, dst, z_s.at[step, s], z_r.at[step, s],
                device_id=(gx, gy, oz), device_id_type=MESH,
            )

        def x_copies(step, d):
            dev = ((gxn if d == 0 else gxp), gy, gz)
            src, dst = ((N + 7, 7), (8, N + 8))[d]
            if step > 0:
                rows = L * PARTS[step - 1][1]
                return [
                    pltpu.make_async_remote_copy(
                        xs.at[step - 1, d, pl.ds(0, rows), :],
                        xr.at[step - 1, d, pl.ds(0, rows), :],
                        x_s.at[step, d, 0], x_r.at[step, d, 0],
                        device_id=dev, device_id_type=MESH,
                    )
                ]
            return [
                pltpu.make_async_remote_copy(
                    tracers.at[:, layer_of(l), pl.ds(src - 8, 1), :],
                    t0.at[:, l + 1, pl.ds(dst, 1), :],
                    x_s.at[0, d, l], x_r.at[0, d, l],
                    device_id=dev, device_id_type=MESH,
                )
                for l in range(L)
            ]

        def y_copy(step, d):
            first, rows = EDGE_ROWS[step]
            return pltpu.make_async_remote_copy(
                ys.at[step, pl.ds(first, rows), :], yr.at[step, d, pl.ds(first, rows), :],
                y_s.at[step, d], y_r.at[step, d],
                device_id=(gx, (gyn if d == 0 else gyp), gz), device_id_type=MESH,
            )

        def m_copy(d):
            src, dst = ((N + 4, 4), (8, N + 8))[d]
            return pltpu.make_async_remote_copy(
                m.at[:, :, pl.ds(src, 4), :], m.at[:, :, pl.ds(dst, 4), :],
                m_s.at[d], m_r.at[d],
                device_id=((gxn if d == 0 else gxp), gy, gz), device_id_type=MESH,
            )

        def send_x(step, when=x_has):
            for d in range(2):
                @pl.when(when[d])
                def _():
                    for c in x_copies(step, d):
                        c.start()

        def recv_x(step):
            for d in range(2):
                @pl.when(x_has[1 - d])
                def _():
                    for c in x_copies(step, d):
                        c.wait_recv()

        def recv_y(step):
            for d in range(2):
                pl.when(y_has[1 - d])(lambda: y_copy(step, d).wait_recv())

        def e_copy(s):
            return pltpu.make_async_remote_copy(
                e_own.at[s], e_oth.at[s], e_s.at[s], e_r.at[s],
                device_id=(gx, gy, oz), device_id_type=MESH,
            )

        def er_copy(s, d):
            return pltpu.make_async_remote_copy(
                e_own.at[s, pl.ds(N - 3, 3), :], er.at[d, s, pl.ds(5, 3), :],
                er_s.at[d, s], er_r.at[d, s],
                device_id=(gxn, gy, (gz if d == 0 else oz)), device_id_type=MESH,
            )

        def ec_copy(i):
            dev = ((gx, gyn, gz), (gx, gyn, oz), (gxn, gyn, gz), (gx, gy, oz))[i]
            return pltpu.make_async_remote_copy(
                (ec.at[2] if i == 3 else es), ec.at[i], ec_s.at[i], ec_r.at[i],
                device_id=dev, device_id_type=MESH,
            )

        z_copy(0, 0).start()
        send_x(0, waits_x)
        z_copy(0, 1).start()

        lane = lax.broadcasted_iota(jnp.int32, (CHUNK, N), 1)
        chunks = tuple(range(0, N, CHUNK))

        def pack_y(src, s):
            for r in chunks:
                acc = ypack[pl.ds(r, CHUNK), :]
                for l in range(L):
                    j = 2 * (s * L + l)
                    c = src[s, l + 1, pl.ds(8 + r, CHUNK), :]
                    here = (lane == j + 1) | (lane == j + 2)
                    acc = jnp.where(here, pltpu.roll(c, j + 2, 1), acc)
                ypack[pl.ds(r, CHUNK), :] = acc

        def unpack_y(step):
            row = lax.broadcasted_iota(jnp.int32, (72, N), 0)
            before = yr[step, 0]
            after = yr[step, 1]
            after = jnp.where(row < 48, pltpu.roll(after, 70, 0), after)
            from_before = ((row < 48) & ((row & 1) == 1)) | ((row >= 48) & ((row & 7) < 4))
            both = jnp.where(from_before, before, after)
            yedge[...] = jnp.concatenate([both, jnp.zeros((N - 72, N), f32)], axis=0).T

        def send_y(step):
            ys[step] = ypack[...].T[:72]
            for d in range(2):
                pl.when(y_has[d])(lambda: y_copy(step, d).start())

        flip = (1 - 2 * gz).astype(f32)

        def moved(src, s, l, r, k):
            j = s * L + l
            c = src[s, l + 1, pl.ds(8 + r, CHUNK), :]
            total = c
            u = wv[0, l, pl.ds(r, CHUNK), :]
            total += (k + jnp.maximum(u, 0.0)) * (src[s, l + 1, pl.ds(7 + r, CHUNK), :] - c)
            total += (k - jnp.minimum(u, 0.0)) * (src[s, l + 1, pl.ds(9 + r, CHUNK), :] - c)
            u = wv[1, l, pl.ds(r, CHUNK), :]
            edge = pltpu.roll(yedge[pl.ds(r, CHUNK), :], N - 1 - 2 * j, 1)
            lower = jnp.where(lane == 0, edge, pltpu.roll(c, 1, 1))
            upper = jnp.where(lane == N - 1, edge, pltpu.roll(c, N - 1, 1))
            total += (k + jnp.maximum(u, 0.0)) * (lower - c)
            total += (k - jnp.minimum(u, 0.0)) * (upper - c)
            u = wv[2, l, pl.ds(r, CHUNK), :] * flip
            total += (k + jnp.maximum(u, 0.0)) * (src[s, l, pl.ds(8 + r, CHUNK), :] - c)
            total += (k - jnp.minimum(u, 0.0)) * (src[s, l + 2, pl.ds(8 + r, CHUNK), :] - c)
            return total

        for c in loads_f:
            c.wait()
        passable = 1.0 - floor[0].astype(f32)
        leave = 1.0 - 0.5 * floor[1].astype(f32)
        start = 0.25 * floor[2].astype(f32) * passable
        m[0, 0, pl.ds(8, N), :] = start
        m[1, 0, pl.ds(8, N), :] = passable
        m[2, 0, pl.ds(8, N), :] = leave
        wide = lax.broadcasted_iota(jnp.int32, (N, N), 1)
        acc = jnp.zeros((N, N), f32)
        for i, field in enumerate((start, passable, leave)):
            a = 48 + 8 * i
            acc = jnp.where((wide >= a) & (wide < a + 8), pltpu.roll(field, a + 4, 1), acc)
        ypack[...] = acc
        for c in loads_t:
            c.wait()

        def pack_y0(s, carry):
            pack_y(t0, s)
            return carry

        lax.fori_loop(0, SPECIES, pack_y0, 0)
        for s in range(2, BEFORE):
            z_copy(0, s).start()

        for d in range(2):
            pl.when(speaks_x[d])(lambda: pl.semaphore_wait(here_x.at[d], 1))
        send_x(0, speaks_x)
        for d in range(2):
            pl.when(odd_y & y_has[d])(lambda: pl.semaphore_wait(here_y.at[d], 1))
        send_y(0)
        for s in range(BEFORE, SPECIES):
            z_copy(0, s).start()
        for c in loads_w:
            c.wait()
        load_b.wait()
        recv_y(0)
        unpack_y(0)

        for i in range(3):
            beside = pltpu.roll(yedge[...], N - 52 - 8 * i, 1)
            m[i, 1, pl.ds(8, N), :] = jnp.where((wide < 4) | (wide >= N - 4), beside, 0.0)
        for d in range(2):
            pl.when(x_has[d])(lambda: m_copy(d).start())
        recv_x(0)

        def unpack_x(part):
            first, count = PARTS[part]
            for d, row in enumerate((7, N + 8)):
                @pl.when(x_has[1 - d])
                def _():
                    for j in range(L * count):
                        t1[first + j // L, 1 + j % L, pl.ds(row, 1), :] = xr[part, d, pl.ds(j, 1), :]

        def first(part, s, carry):
            k = coefficient_of(s)
            z_copy(0, s).wait_recv()
            for l in (L - 1, 0, 1, 2):
                for r in chunks:
                    t1[s, l + 1, pl.ds(8 + r, CHUNK), :] = moved(t0, s, l, r, k)

            @pl.when(s != 2)
            def _():
                z_copy(1, s).start()

            pack_y(t1, s)
            for l in range(L):
                j = (s - PARTS[part][0]) * L + l
                xs[part, 0, pl.ds(j, 1), :] = t1[s, l + 1, pl.ds(N + 7, 1), :]
                xs[part, 1, pl.ds(j, 1), :] = t1[s, l + 1, pl.ds(8, 1), :]
            return carry

        lax.fori_loop(0, 3, functools.partial(first, 0), 0)
        send_x(1)
        send_y(1)
        z_copy(1, 2).start()
        lax.fori_loop(3, SPECIES, functools.partial(first, 1), 0)
        send_x(2)
        send_y(2)

        for d in range(2):
            pl.when(x_has[1 - d])(lambda: m_copy(d).wait_recv())
        rows = N + 16
        lane_m = lax.broadcasted_iota(jnp.int32, (rows, N), 1)

        def y_lower(a, b):
            ra, rb = pltpu.roll(a, 1, 1), pltpu.roll(b, 1, 1)
            return jnp.where(lane_m == 0, rb, ra), jnp.where(lane_m == 0, ra, rb)

        def y_upper(a, b):
            ra, rb = pltpu.roll(a, N - 1, 1), pltpu.roll(b, N - 1, 1)
            return jnp.where(lane_m == N - 1, rb, ra), jnp.where(lane_m == N - 1, ra, rb)

        occ = [m[0, i] for i in range(2)]
        free = [m[1, i] for i in range(2)]
        out = [m[2, i] for i in range(2)]
        free_y = y_upper(*free)
        px = [0.25 * free[i] * pltpu.roll(free[i], rows - 1, 0) for i in range(2)]
        py = [0.15 * free[i] * free_y[i] for i in range(2)]
        for step in range(4):
            occ_yu = y_upper(*occ)
            occ_yl = y_lower(*occ)
            gate_x = [px[i] * (1.0 - pltpu.roll(occ[i], rows - 1, 0)) for i in range(2)]
            gate_y = [py[i] * (1.0 - occ_yu[i]) for i in range(2)]
            gate_yl = y_lower(*gate_y)
            after = []
            for i in range(2):
                stay = out[i] * (1.0 - gate_x[i] - gate_y[i])
                in_x = out[i] * pltpu.roll(gate_x[i], 1, 0)
                in_y = out[i] * gate_yl[i]
                c0[step, i] = stay[: N + 8]
                cx[step, i] = in_x[: N + 8]
                cy[step, i] = in_y[: N + 8]
                co[step, i] = (out[i] * occ[i])[: N + 8]
                after.append(stay * occ[i] + in_x * pltpu.roll(occ[i], 1, 0) + in_y * occ_yl[i])
            occ = after
        out_o[...] = occ[0][8 : N + 8]

        recv_x(1)
        unpack_x(0)
        recv_y(1)
        unpack_y(1)

        def in_band(l, r):
            b = band[pl.ds(r, CHUNK), :]
            layer = l * oz + (2 * L - 1 - l) * gz
            return (b == layer) | (b == layer - 1)

        def second(s, carry):
            k = coefficient_of(s)
            for r in chunks:
                acc = jnp.zeros((CHUNK, N), f32)
                for l in range(L - 1):
                    new = moved(t1, s, l, r, k)
                    out_t[s, layer_of(l), pl.ds(r, CHUNK), :] = new
                    acc += jnp.where(in_band(l, r), 0.5 * new, 0.0)
                e_own[s, pl.ds(r, CHUNK), :] = acc
            z_copy(1, s).wait_recv()
            for r in chunks:
                new = moved(t1, s, L - 1, r, k)
                out_t[s, boundary, pl.ds(r, CHUNK), :] = new
                e_own[s, pl.ds(r, CHUNK), :] += jnp.where(in_band(L - 1, r), 0.5 * new, 0.0)

            @pl.when(has_xn)
            def _():
                er_copy(s, 0).start()
                er_copy(s, 1).start()

            @pl.when(s < HOLD)
            def _():
                e_copy(s).start()

            return carry

        lax.fori_loop(0, 3, second, 0)
        recv_x(2)
        unpack_x(1)
        recv_y(2)
        unpack_y(2)
        lax.fori_loop(3, SPECIES, second, 0)
        strip = jnp.zeros((N, N), f32)
        for s in range(SPECIES):
            mine = (wide >= 3 * s) & (wide < 3 * s + 3)
            strip = jnp.where(mine, pltpu.roll(e_own[s], 3 * s + 3, 1), strip)
        es[...] = strip.T[:16]
        ec_to = (has_yn, has_yn, has_xn & has_yn, has_xp & has_yp)
        ec_from = (has_yp, has_yp, has_xp & has_yp, has_xp & has_yp)
        for i in range(3):
            pl.when(ec_to[i])(lambda: ec_copy(i).start())
        for s in range(HOLD, SPECIES):
            e_copy(s).start()

        def rate_of(co_, co2, hcn, o2, heat):
            return (
                0.3 * co_ * jnp.exp(0.3 * co2) + 0.2 * hcn
                + 0.1 * (2.0 - o2) * (2.0 - o2) + 0.1 * heat * heat
            )

        @pl.when(has_xp)
        def _():
            for s in range(SPECIES):
                er_copy(s, 0).wait_recv()
                er_copy(s, 1).wait_recv()

        edge = rate_of(*[er[0, s] + er[1, s] for s in range(SPECIES)])
        for i in range(3):
            pl.when(ec_from[i])(lambda: ec_copy(i).wait_recv())
        pl.when(ec_from[3])(lambda: ec_copy(3).start())
        pl.when(ec_from[3])(lambda: ec_copy(3).wait_recv())
        filler = jnp.zeros((N - 16, N), f32)
        side = jnp.concatenate([ec[0] + ec[1], filler], axis=0).T
        corner = jnp.concatenate([ec[2] + ec[3], filler], axis=0).T[N - 8 :]
        side = jnp.concatenate([corner, side], axis=0)
        side = rate_of(*[pltpu.roll(side, N - 3 - 3 * s, 1) for s in range(SPECIES)])
        for s in range(SPECIES):
            e_copy(s).wait_recv()
        middle = rate_of(*[e_own[s] + e_oth[s] for s in range(SPECIES)])
        lane_d = lax.broadcasted_iota(jnp.int32, (N + 8, N), 1)
        out_rate[0, pl.ds(0, 8), :] = edge
        out_rate[0, pl.ds(8, N), :] = middle
        out_rate[1] = jnp.where(lane_d >= N - 3, side, 0.0)

        for d in range(2):
            @pl.when(x_has[d])
            def _():
                for step in range(3):
                    for c in x_copies(step, d):
                        c.wait_send()
                m_copy(d).wait_send()

            @pl.when(y_has[d])
            def _():
                for step in range(3):
                    y_copy(step, d).wait_send()

        for s in range(SPECIES):
            z_copy(0, s).wait_send()
            z_copy(1, s).wait_send()
            e_copy(s).wait_send()

        @pl.when(has_xn)
        def _():
            for s in range(SPECIES):
                er_copy(s, 0).wait_send()
                er_copy(s, 1).wait_send()

        for i in range(4):
            pl.when(ec_to[i])(lambda: ec_copy(i).wait_send())

    return kernel


def finish(fields, occupants, c0, cx, cy, co, rate, out_t, out_o, out_f, dose_v, sem_t, sem_o, sem_f):
    copies = [
        pltpu.make_async_copy(fields.at[s], out_t.at[s], sem_t.at[s]) for s in range(SPECIES)
    ]
    copies.append(pltpu.make_async_copy(occupants, out_o, sem_o))
    for c in copies:
        c.start()
    lane = lax.broadcasted_iota(jnp.int32, (N + 8, N), 1)
    dose = [co[0, i] * rate[i] for i in range(2)]
    for step in range(1, 4):
        ra, rb = pltpu.roll(dose[0], 1, 1), pltpu.roll(dose[1], 1, 1)
        left = (jnp.where(lane == 0, rb, ra), jnp.where(lane == 0, ra, rb))
        dose = [
            c0[step, i] * dose[i] + cx[step, i] * pltpu.roll(dose[i], 1, 0)
            + cy[step, i] * left[i] + co[step, i] * rate[i]
            for i in range(2)
        ]
    dose_v[...] = dose[0][8:]
    copies.append(pltpu.make_async_copy(dose_v, out_f, sem_f))
    copies[-1].start()
    for c in copies:
        c.wait()


def solution(mesh):
    sizes = tuple(mesh.shape[name] for name in ("gx", "gy", "gz"))

    def on_device(tracers, wind_field, band_layer, wall_mask, exit_mask, occupant_count):
        floor = jax.ShapeDtypeStruct((N, N), f32)
        hbm = pl.BlockSpec(memory_space=pltpu.HBM)
        vmem = pl.BlockSpec(memory_space=pltpu.VMEM)
        V = pltpu.VMEM
        D = pltpu.SemaphoreType.DMA
        R = pltpu.SemaphoreType.REGULAR
        weights = jax.ShapeDtypeStruct((4, 2, N + 8, N), f32)
        cells = jax.ShapeDtypeStruct((SPECIES, L, N, N), f32)
        found = pl.pallas_call(
            make_kernel(sizes),
            out_shape=(
                cells, floor, weights, weights, weights, weights,
                jax.ShapeDtypeStruct((2, N + 8, N), f32),
            ),
            in_specs=[hbm] * 6,
            out_specs=(vmem,) * 7,
            scratch_shapes=[
                V((SPECIES, L + 2, N + 16, N), f32),
                V((SPECIES, L + 2, N + 16, N), f32),
                V((3, L, N, N), f32),
                V((N, N), jnp.int32),
                V((3, N, N), jnp.int32),
                V((N, N), f32), V((N, N), f32),
                V((3, 72, N), f32), V((3, 2, 72, N), f32),
                V((2, 2, 16, N), f32), V((2, 2, 16, N), f32),
                V((3, 2, N + 16, N), f32),
                V((SPECIES, N, N), f32), V((SPECIES, N, N), f32),
                V((2, SPECIES, 8, N), f32),
                V((16, N), f32), V((4, 16, N), f32),
                D((L,)), D((L,)), D, D((3,)),
                D((2, SPECIES)), D((2, SPECIES)),
                D((3, 2, L)), D((3, 2, L)), D((3, 2)), D((3, 2)), D((2,)), D((2,)),
                D((SPECIES,)), D((SPECIES,)), D((2, SPECIES)), D((2, SPECIES)),
                D((4,)), D((4,)),
                R((2,)), R((2,)),
            ],
            compiler_params=pltpu.CompilerParams(
                collective_id=0, has_side_effects=True, vmem_limit_bytes=32 * 1024 * 1024
            ),
        )(*[pltpu.with_memory_space_constraint(a, pltpu.HBM) for a in (tracers, wind_field, band_layer, wall_mask, exit_mask, occupant_count)])
        return pl.pallas_call(
            finish,
            out_shape=(cells, floor, floor),
            in_specs=[vmem] * 7,
            out_specs=(hbm,) * 3,
            scratch_shapes=[V((N, N), f32), D((SPECIES,)), D, D],
            compiler_params=pltpu.CompilerParams(vmem_limit_bytes=16 * 1024 * 1024),
        )(*found)

    return jax.shard_map(
        on_device,
        mesh=mesh,
        in_specs=(
            P(None, "gz", "gx", "gy"),
            P(None, "gz", "gx", "gy"),
            P("gx", "gy"),
            P("gx", "gy"),
            P("gx", "gy"),
            P("gx", "gy"),
        ),
        out_specs=(P(None, "gz", "gx", "gy"), P("gx", "gy"), P("gx", "gy")),
        check_vma=False,
    )
```

```python
import functools

import jax
import jax.numpy as jnp
from jax import lax
from jax.experimental import pallas as pl
from jax.experimental.pallas import tpu as pltpu
from jax.sharding import PartitionSpec as P

diffusivity = (0.05, 0.04, 0.06, 0.03, 0.045)
SPECIES = 5
L = 4
N = 128
CHUNK = 32
HOLD = 3
BEFORE = 4
PARTS = ((0, 3), (3, 2))
EDGE_ROWS = ((0, 72), (0, 32), (24, 24))
MESH = pl.DeviceIdType.MESH
f32 = jnp.float32


def coefficient_of(s):
    k = jnp.float32(diffusivity[0])
    for i in range(1, SPECIES):
        k = jnp.where(s == i, jnp.float32(diffusivity[i]), k)
    return k


def make_kernel(sizes):
    nx, ny, nz = sizes

    def kernel(
        tracers, wind, band_in, wall_in, exit_in, count_in,
        out_t, out_o, c0, cx, cy, co, out_rate,
        t0, t1, wv, band, floor,
        yedge, ypack, middle, ys, yr, xs, xr,
        m,
        e_own, e_oth, er, es, ec,
        sem_t, sem_w, sem_b, sem_f,
        z_s, z_r, x_s, x_r, y_s, y_r, m_s, m_r,
        e_s, e_r, er_s, er_r, ec_s, ec_r, here_x, here_y,
    ):
        gx, gy, gz = lax.axis_index("gx"), lax.axis_index("gy"), lax.axis_index("gz")
        oz = 1 - gz
        gxn, gxp, gyn, gyp = gx + 1, gx - 1, gy + 1, gy - 1
        has_xn, has_xp, has_yn, has_yp = gx < nx - 1, gx > 0, gy < ny - 1, gy > 0
        x_has = (has_xn, has_xp)
        y_has = (has_yn, has_yp)
        boundary = (L - 1) * oz

        def layer_of(l):
            return l * oz + (L - 1 - l) * gz

        loads_t = [
            pltpu.make_async_copy(
                tracers.at[:, layer_of(l)], t0.at[:, l + 1, pl.ds(8, N), :], sem_t.at[l]
            )
            for l in range(L)
        ]
        loads_w = [
            pltpu.make_async_copy(wind.at[:, layer_of(l)], wv.at[:, l], sem_w.at[l])
            for l in range(L)
        ]
        loads_f = [
            pltpu.make_async_copy(ref, floor.at[i], sem_f.at[i])
            for i, ref in enumerate((wall_in, exit_in, count_in))
        ]
        load_b = pltpu.make_async_copy(band_in, band, sem_b)
        for c in loads_t:
            c.start()
        for c in loads_f:
            c.start()
        for c in loads_w:
            c.start()
        load_b.start()

        barrier = pltpu.get_barrier_semaphore()

        def greet(*devs):
            for dev in devs:
                pl.semaphore_signal(barrier, inc=1, device_id=dev, device_id_type=MESH)

        greet((gx, gy, oz))
        odd_y, even_y = lax.rem(gy, 2) == 1, lax.rem(gy, 2) == 0
        speaks_x = ((gx > 0) & has_xn, gx == 1)
        waits_x = ((gx == 0) & has_xn, gx > 1)
        x_dev = ((gxn, gy, gz), (gxp, gy, gz))
        y_dev = ((gx, gyn, gz), (gx, gyp, gz))
        for d in range(2):
            pl.when(speaks_x[d])(lambda: greet(x_dev[d]))
            pl.when(odd_y & y_has[d])(lambda: greet(y_dev[d]))

        def clear(s, carry):
            t0[s, 0, pl.ds(8, N), :] = jnp.zeros((N, N), f32)
            t1[s, 0, pl.ds(8, N), :] = jnp.zeros((N, N), f32)
            return carry

        lax.fori_loop(0, SPECIES, clear, 0)

        def clear_rows(row):
            for s in range(SPECIES):
                for l in range(1, L + 1):
                    t0[s, l, pl.ds(row, 1), :] = jnp.zeros((1, N), f32)
                    t1[s, l, pl.ds(row, 1), :] = jnp.zeros((1, N), f32)

        er[:, :, pl.ds(0, 5), :] = jnp.zeros((2, SPECIES, 5, N), f32)
        m[:, :, pl.ds(0, 4), :] = jnp.zeros((3, 2, 4, N), f32)
        m[:, :, pl.ds(N + 12, 4), :] = jnp.zeros((3, 2, 4, N), f32)

        @pl.when(jnp.logical_not(has_xp))
        def _():
            clear_rows(7)
            er[:, :, pl.ds(5, 3), :] = jnp.zeros((2, SPECIES, 3, N), f32)
            m[:, :, pl.ds(4, 4), :] = jnp.zeros((3, 2, 4, N), f32)

        @pl.when(jnp.logical_not(has_xn))
        def _():
            clear_rows(N + 8)
            m[:, :, pl.ds(N + 8, 4), :] = jnp.zeros((3, 2, 4, N), f32)

        @pl.when(jnp.logical_not(has_yp))
        def _():
            for step in range(3):
                yr[step, 0] = jnp.zeros((72, N), f32)
            ec[0] = jnp.zeros((16, N), f32)
            ec[1] = jnp.zeros((16, N), f32)

        @pl.when(jnp.logical_not(has_yn))
        def _():
            for step in range(3):
                yr[step, 1] = jnp.zeros((72, N), f32)

        @pl.when(jnp.logical_not(has_xp & has_yp))
        def _():
            ec[2] = jnp.zeros((16, N), f32)
            ec[3] = jnp.zeros((16, N), f32)

        one = lambda flag: flag.astype(jnp.int32)
        pl.semaphore_wait(
            barrier,
            1 + one(waits_x[0]) + one(waits_x[1])
            + one(even_y) * (one(has_yn) + one(has_yp)),
        )

        def answer(sem, dev):
            pl.semaphore_signal(sem, inc=1, device_id=dev, device_id_type=MESH)

        for d in range(2):
            pl.when(waits_x[d])(lambda: answer(here_x.at[1 - d], x_dev[d]))
            pl.when(even_y & y_has[d])(lambda: answer(here_y.at[1 - d], y_dev[d]))

        def z_copy(step, s):
            src = tracers.at[s, boundary] if step == 0 else t1.at[s, L, pl.ds(8, N), :]
            dst = (t0 if step == 0 else t1).at[s, L + 1, pl.ds(8, N), :]
            return pltpu.make_async_remote_copy(
                src, dst, z_s.at[step, s], z_r.at[step, s],
                device_id=(gx, gy, oz), device_id_type=MESH,
            )

        def x_copies(step, d):
            dev = ((gxn if d == 0 else gxp), gy, gz)
            src, dst = ((N + 7, 7), (8, N + 8))[d]
            if step > 0:
                rows = L * PARTS[step - 1][1]
                return [
                    pltpu.make_async_remote_copy(
                        xs.at[step - 1, d, pl.ds(0, rows), :],
                        xr.at[step - 1, d, pl.ds(0, rows), :],
                        x_s.at[step, d, 0], x_r.at[step, d, 0],
                        device_id=dev, device_id_type=MESH,
                    )
                ]
            return [
                pltpu.make_async_remote_copy(
                    tracers.at[:, layer_of(l), pl.ds(src - 8, 1), :],
                    t0.at[:, l + 1, pl.ds(dst, 1), :],
                    x_s.at[0, d, l], x_r.at[0, d, l],
                    device_id=dev, device_id_type=MESH,
                )
                for l in range(L)
            ]

        def y_copy(step, d):
            first, rows = EDGE_ROWS[step]
            return pltpu.make_async_remote_copy(
                ys.at[step, pl.ds(first, rows), :], yr.at[step, d, pl.ds(first, rows), :],
                y_s.at[step, d], y_r.at[step, d],
                device_id=(gx, (gyn if d == 0 else gyp), gz), device_id_type=MESH,
            )

        def m_copy(d):
            src, dst = ((N + 4, 4), (8, N + 8))[d]
            return pltpu.make_async_remote_copy(
                m.at[:, :, pl.ds(src, 4), :], m.at[:, :, pl.ds(dst, 4), :],
                m_s.at[d], m_r.at[d],
                device_id=((gxn if d == 0 else gxp), gy, gz), device_id_type=MESH,
            )

        def send_x(step, when=x_has):
            for d in range(2):
                @pl.when(when[d])
                def _():
                    for c in x_copies(step, d):
                        c.start()

        def recv_x(step):
            for d in range(2):
                @pl.when(x_has[1 - d])
                def _():
                    for c in x_copies(step, d):
                        c.wait_recv()

        def recv_y(step):
            for d in range(2):
                pl.when(y_has[1 - d])(lambda: y_copy(step, d).wait_recv())

        def e_copy(s):
            return pltpu.make_async_remote_copy(
                e_own.at[s], e_oth.at[s], e_s.at[s], e_r.at[s],
                device_id=(gx, gy, oz), device_id_type=MESH,
            )

        def er_copy(s, d):
            return pltpu.make_async_remote_copy(
                e_own.at[s, pl.ds(N - 3, 3), :], er.at[d, s, pl.ds(5, 3), :],
                er_s.at[d, s], er_r.at[d, s],
                device_id=(gxn, gy, (gz if d == 0 else oz)), device_id_type=MESH,
            )

        def ec_copy(i):
            dev = ((gx, gyn, gz), (gx, gyn, oz), (gxn, gyn, gz), (gx, gy, oz))[i]
            return pltpu.make_async_remote_copy(
                (ec.at[2] if i == 3 else es), ec.at[i], ec_s.at[i], ec_r.at[i],
                device_id=dev, device_id_type=MESH,
            )

        z_copy(0, 0).start()
        send_x(0, waits_x)
        z_copy(0, 1).start()

        lane = lax.broadcasted_iota(jnp.int32, (CHUNK, N), 1)
        chunks = tuple(range(0, N, CHUNK))

        def pack_y(src, s):
            for r in chunks:
                acc = ypack[pl.ds(r, CHUNK), :]
                for l in range(L):
                    j = 2 * (s * L + l)
                    c = src[s, l + 1, pl.ds(8 + r, CHUNK), :]
                    here = (lane == j + 1) | (lane == j + 2)
                    acc = jnp.where(here, pltpu.roll(c, j + 2, 1), acc)
                ypack[pl.ds(r, CHUNK), :] = acc

        def unpack_y(step):
            row = lax.broadcasted_iota(jnp.int32, (72, N), 0)
            before = yr[step, 0]
            after = yr[step, 1]
            after = jnp.where(row < 48, pltpu.roll(after, 70, 0), after)
            from_before = ((row < 48) & ((row & 1) == 1)) | ((row >= 48) & ((row & 7) < 4))
            both = jnp.where(from_before, before, after)
            yedge[...] = jnp.concatenate([both, jnp.zeros((N - 72, N), f32)], axis=0).T

        def send_y(step):
            ys[step] = ypack[...].T[:72]
            for d in range(2):
                pl.when(y_has[d])(lambda: y_copy(step, d).start())

        flip = (1 - 2 * gz).astype(f32)

        def moved(src, s, l, r, k):
            j = s * L + l
            c = src[s, l + 1, pl.ds(8 + r, CHUNK), :]
            total = c
            u = wv[0, l, pl.ds(r, CHUNK), :]
            total += (k + jnp.maximum(u, 0.0)) * (src[s, l + 1, pl.ds(7 + r, CHUNK), :] - c)
            total += (k - jnp.minimum(u, 0.0)) * (src[s, l + 1, pl.ds(9 + r, CHUNK), :] - c)
            u = wv[1, l, pl.ds(r, CHUNK), :]
            edge = pltpu.roll(yedge[pl.ds(r, CHUNK), :], N - 1 - 2 * j, 1)
            lower = jnp.where(lane == 0, edge, pltpu.roll(c, 1, 1))
            upper = jnp.where(lane == N - 1, edge, pltpu.roll(c, N - 1, 1))
            total += (k + jnp.maximum(u, 0.0)) * (lower - c)
            total += (k - jnp.minimum(u, 0.0)) * (upper - c)
            u = wv[2, l, pl.ds(r, CHUNK), :] * flip
            total += (k + jnp.maximum(u, 0.0)) * (src[s, l, pl.ds(8 + r, CHUNK), :] - c)
            total += (k - jnp.minimum(u, 0.0)) * (src[s, l + 2, pl.ds(8 + r, CHUNK), :] - c)
            return total

        for c in loads_f:
            c.wait()
        passable = 1.0 - floor[0].astype(f32)
        leave = 1.0 - 0.5 * floor[1].astype(f32)
        start = 0.25 * floor[2].astype(f32) * passable
        m[0, 0, pl.ds(8, N), :] = start
        m[1, 0, pl.ds(8, N), :] = passable
        m[2, 0, pl.ds(8, N), :] = leave
        wide = lax.broadcasted_iota(jnp.int32, (N, N), 1)
        acc = jnp.zeros((N, N), f32)
        for i, field in enumerate((start, passable, leave)):
            a = 48 + 8 * i
            acc = jnp.where((wide >= a) & (wide < a + 8), pltpu.roll(field, a + 4, 1), acc)
        ypack[...] = acc
        for c in loads_t:
            c.wait()

        def pack_y0(s, carry):
            pack_y(t0, s)
            return carry

        lax.fori_loop(0, SPECIES, pack_y0, 0)
        for s in range(2, BEFORE):
            z_copy(0, s).start()

        for d in range(2):
            pl.when(speaks_x[d])(lambda: pl.semaphore_wait(here_x.at[d], 1))
        send_x(0, speaks_x)
        for d in range(2):
            pl.when(odd_y & y_has[d])(lambda: pl.semaphore_wait(here_y.at[d], 1))
        send_y(0)
        for s in range(BEFORE, SPECIES):
            z_copy(0, s).start()
        for c in loads_w:
            c.wait()
        load_b.wait()
        recv_y(0)
        unpack_y(0)

        for i in range(3):
            beside = pltpu.roll(yedge[...], N - 52 - 8 * i, 1)
            m[i, 1, pl.ds(8, N), :] = jnp.where((wide < 4) | (wide >= N - 4), beside, 0.0)
        for d in range(2):
            pl.when(x_has[d])(lambda: m_copy(d).start())
        recv_x(0)

        def unpack_x(part):
            first, count = PARTS[part]
            for d, row in enumerate((7, N + 8)):
                @pl.when(x_has[1 - d])
                def _():
                    for j in range(L * count):
                        t1[first + j // L, 1 + j % L, pl.ds(row, 1), :] = xr[part, d, pl.ds(j, 1), :]

        def first(part, s, carry):
            k = coefficient_of(s)
            z_copy(0, s).wait_recv()
            for l in (L - 1, 0, 1, 2):
                for r in chunks:
                    t1[s, l + 1, pl.ds(8 + r, CHUNK), :] = moved(t0, s, l, r, k)

            @pl.when(s != 2)
            def _():
                z_copy(1, s).start()

            pack_y(t1, s)
            for l in range(L):
                j = (s - PARTS[part][0]) * L + l
                xs[part, 0, pl.ds(j, 1), :] = t1[s, l + 1, pl.ds(N + 7, 1), :]
                xs[part, 1, pl.ds(j, 1), :] = t1[s, l + 1, pl.ds(8, 1), :]
            return carry

        lax.fori_loop(0, 3, functools.partial(first, 0), 0)
        send_x(1)
        send_y(1)
        z_copy(1, 2).start()
        lax.fori_loop(3, SPECIES, functools.partial(first, 1), 0)
        send_x(2)
        send_y(2)

        for d in range(2):
            pl.when(x_has[1 - d])(lambda: m_copy(d).wait_recv())
        rows = N + 16
        lane_m = lax.broadcasted_iota(jnp.int32, (rows, N), 1)

        def y_lower(a, b):
            ra, rb = pltpu.roll(a, 1, 1), pltpu.roll(b, 1, 1)
            return jnp.where(lane_m == 0, rb, ra), jnp.where(lane_m == 0, ra, rb)

        def y_upper(a, b):
            ra, rb = pltpu.roll(a, N - 1, 1), pltpu.roll(b, N - 1, 1)
            return jnp.where(lane_m == N - 1, rb, ra), jnp.where(lane_m == N - 1, ra, rb)

        occ = [m[0, i] for i in range(2)]
        free = [m[1, i] for i in range(2)]
        out = [m[2, i] for i in range(2)]
        free_y = y_upper(*free)
        px = [0.25 * free[i] * pltpu.roll(free[i], rows - 1, 0) for i in range(2)]
        py = [0.15 * free[i] * free_y[i] for i in range(2)]
        for step in range(4):
            occ_yu = y_upper(*occ)
            occ_yl = y_lower(*occ)
            gate_x = [px[i] * (1.0 - pltpu.roll(occ[i], rows - 1, 0)) for i in range(2)]
            gate_y = [py[i] * (1.0 - occ_yu[i]) for i in range(2)]
            gate_yl = y_lower(*gate_y)
            after = []
            for i in range(2):
                stay = out[i] * (1.0 - gate_x[i] - gate_y[i])
                in_x = out[i] * pltpu.roll(gate_x[i], 1, 0)
                in_y = out[i] * gate_yl[i]
                c0[step, i] = stay[: N + 8]
                cx[step, i] = in_x[: N + 8]
                cy[step, i] = in_y[: N + 8]
                co[step, i] = (out[i] * occ[i])[: N + 8]
                after.append(stay * occ[i] + in_x * pltpu.roll(occ[i], 1, 0) + in_y * occ_yl[i])
            occ = after
        out_o[...] = occ[0][8 : N + 8]

        recv_x(1)
        unpack_x(0)
        recv_y(1)
        unpack_y(1)

        def in_band(l, r):
            b = band[pl.ds(r, CHUNK), :]
            layer = l * oz + (2 * L - 1 - l) * gz
            return (b == layer) | (b == layer - 1)

        def second(s, carry):
            k = coefficient_of(s)
            for r in chunks:
                acc = jnp.zeros((CHUNK, N), f32)
                for l in range(L - 1):
                    new = moved(t1, s, l, r, k)
                    out_t[s, layer_of(l), pl.ds(r, CHUNK), :] = new
                    acc += jnp.where(in_band(l, r), 0.5 * new, 0.0)
                e_own[s, pl.ds(r, CHUNK), :] = acc
            z_copy(1, s).wait_recv()
            for r in chunks:
                new = moved(t1, s, L - 1, r, k)
                out_t[s, boundary, pl.ds(r, CHUNK), :] = new
                e_own[s, pl.ds(r, CHUNK), :] += jnp.where(in_band(L - 1, r), 0.5 * new, 0.0)

            @pl.when(has_xn)
            def _():
                er_copy(s, 0).start()
                er_copy(s, 1).start()

            @pl.when(s < HOLD)
            def _():
                e_copy(s).start()

            return carry

        lax.fori_loop(0, 3, second, 0)
        recv_x(2)
        unpack_x(1)
        recv_y(2)
        unpack_y(2)
        lax.fori_loop(3, SPECIES, second, 0)
        strip = jnp.zeros((N, N), f32)
        for s in range(SPECIES):
            mine = (wide >= 3 * s) & (wide < 3 * s + 3)
            strip = jnp.where(mine, pltpu.roll(e_own[s], 3 * s + 3, 1), strip)
        es[...] = strip.T[:16]
        ec_to = (has_yn, has_yn, has_xn & has_yn, has_xp & has_yp)
        ec_from = (has_yp, has_yp, has_xp & has_yp, has_xp & has_yp)
        for i in range(3):
            pl.when(ec_to[i])(lambda: ec_copy(i).start())
        for s in range(HOLD, SPECIES):
            e_copy(s).start()

        def rate_of(co_, co2, hcn, o2, heat):
            return (
                0.3 * co_ * jnp.exp(0.3 * co2) + 0.2 * hcn
                + 0.1 * (2.0 - o2) * (2.0 - o2) + 0.1 * heat * heat
            )

        @pl.when(has_xp)
        def _():
            for s in range(SPECIES):
                er_copy(s, 0).wait_recv()
                er_copy(s, 1).wait_recv()

        edge = rate_of(*[er[0, s] + er[1, s] for s in range(SPECIES)])
        for i in range(3):
            pl.when(ec_from[i])(lambda: ec_copy(i).wait_recv())
        pl.when(ec_from[3])(lambda: ec_copy(3).start())
        pl.when(ec_from[3])(lambda: ec_copy(3).wait_recv())
        filler = jnp.zeros((N - 16, N), f32)
        side = jnp.concatenate([ec[0] + ec[1], filler], axis=0).T
        corner = jnp.concatenate([ec[2] + ec[3], filler], axis=0).T[N - 8 :]
        side = jnp.concatenate([corner, side], axis=0)
        side = rate_of(*[pltpu.roll(side, N - 3 - 3 * s, 1) for s in range(SPECIES)])
        out_rate[0, pl.ds(0, 8), :] = edge
        for s in range(SPECIES - 1):
            e_copy(s).wait_recv()
        lane_d = lax.broadcasted_iota(jnp.int32, (N + 8, N), 1)
        out_rate[1] = jnp.where(lane_d >= N - 3, side, 0.0)
        zero = jnp.zeros((N, N), f32)
        middle[...] = rate_of(*[e_own[s] + e_oth[s] for s in range(SPECIES - 1)], zero)
        e_copy(SPECIES - 1).wait_recv()
        heat = e_own[SPECIES - 1] + e_oth[SPECIES - 1]
        out_rate[0, pl.ds(8, N), :] = middle[...] + 0.1 * heat * heat

        for d in range(2):
            @pl.when(x_has[d])
            def _():
                for step in range(3):
                    for c in x_copies(step, d):
                        c.wait_send()
                m_copy(d).wait_send()

            @pl.when(y_has[d])
            def _():
                for step in range(3):
                    y_copy(step, d).wait_send()

        for s in range(SPECIES):
            z_copy(0, s).wait_send()
            z_copy(1, s).wait_send()
            e_copy(s).wait_send()

        @pl.when(has_xn)
        def _():
            for s in range(SPECIES):
                er_copy(s, 0).wait_send()
                er_copy(s, 1).wait_send()

        for i in range(4):
            pl.when(ec_to[i])(lambda: ec_copy(i).wait_send())

    return kernel


def finish(fields, occupants, c0, cx, cy, co, rate, out_t, out_o, out_f, dose_v, sem_t, sem_o, sem_f):
    copies = [
        pltpu.make_async_copy(fields.at[s], out_t.at[s], sem_t.at[s]) for s in range(SPECIES)
    ]
    copies.append(pltpu.make_async_copy(occupants, out_o, sem_o))
    for c in copies:
        c.start()
    lane = lax.broadcasted_iota(jnp.int32, (N + 8, N), 1)
    dose = [co[0, i] * rate[i] for i in range(2)]
    for step in range(1, 4):
        ra, rb = pltpu.roll(dose[0], 1, 1), pltpu.roll(dose[1], 1, 1)
        left = (jnp.where(lane == 0, rb, ra), jnp.where(lane == 0, ra, rb))
        dose = [
            c0[step, i] * dose[i] + cx[step, i] * pltpu.roll(dose[i], 1, 0)
            + cy[step, i] * left[i] + co[step, i] * rate[i]
            for i in range(2)
        ]
    dose_v[...] = dose[0][8:]
    copies.append(pltpu.make_async_copy(dose_v, out_f, sem_f))
    copies[-1].start()
    for c in copies:
        c.wait()


def solution(mesh):
    sizes = tuple(mesh.shape[name] for name in ("gx", "gy", "gz"))

    def on_device(tracers, wind_field, band_layer, wall_mask, exit_mask, occupant_count):
        floor = jax.ShapeDtypeStruct((N, N), f32)
        hbm = pl.BlockSpec(memory_space=pltpu.HBM)
        vmem = pl.BlockSpec(memory_space=pltpu.VMEM)
        V = pltpu.VMEM
        D = pltpu.SemaphoreType.DMA
        R = pltpu.SemaphoreType.REGULAR
        weights = jax.ShapeDtypeStruct((4, 2, N + 8, N), f32)
        cells = jax.ShapeDtypeStruct((SPECIES, L, N, N), f32)
        found = pl.pallas_call(
            make_kernel(sizes),
            out_shape=(
                cells, floor, weights, weights, weights, weights,
                jax.ShapeDtypeStruct((2, N + 8, N), f32),
            ),
            in_specs=[hbm] * 6,
            out_specs=(vmem,) * 7,
            scratch_shapes=[
                V((SPECIES, L + 2, N + 16, N), f32),
                V((SPECIES, L + 2, N + 16, N), f32),
                V((3, L, N, N), f32),
                V((N, N), jnp.int32),
                V((3, N, N), jnp.int32),
                V((N, N), f32), V((N, N), f32), V((N, N), f32),
                V((3, 72, N), f32), V((3, 2, 72, N), f32),
                V((2, 2, 16, N), f32), V((2, 2, 16, N), f32),
                V((3, 2, N + 16, N), f32),
                V((SPECIES, N, N), f32), V((SPECIES, N, N), f32),
                V((2, SPECIES, 8, N), f32),
                V((16, N), f32), V((4, 16, N), f32),
                D((L,)), D((L,)), D, D((3,)),
                D((2, SPECIES)), D((2, SPECIES)),
                D((3, 2, L)), D((3, 2, L)), D((3, 2)), D((3, 2)), D((2,)), D((2,)),
                D((SPECIES,)), D((SPECIES,)), D((2, SPECIES)), D((2, SPECIES)),
                D((4,)), D((4,)),
                R((2,)), R((2,)),
            ],
            compiler_params=pltpu.CompilerParams(
                collective_id=0, has_side_effects=True, vmem_limit_bytes=32 * 1024 * 1024
            ),
        )(*[pltpu.with_memory_space_constraint(a, pltpu.HBM) for a in (tracers, wind_field, band_layer, wall_mask, exit_mask, occupant_count)])
        return pl.pallas_call(
            finish,
            out_shape=(cells, floor, floor),
            in_specs=[vmem] * 7,
            out_specs=(hbm,) * 3,
            scratch_shapes=[V((N, N), f32), D((SPECIES,)), D, D],
            compiler_params=pltpu.CompilerParams(vmem_limit_bytes=16 * 1024 * 1024),
        )(*found)

    return jax.shard_map(
        on_device,
        mesh=mesh,
        in_specs=(
            P(None, "gz", "gx", "gy"),
            P(None, "gz", "gx", "gy"),
            P("gx", "gy"),
            P("gx", "gy"),
            P("gx", "gy"),
            P("gx", "gy"),
        ),
        out_specs=(P(None, "gz", "gx", "gy"), P("gx", "gy"), P("gx", "gy")),
        check_vma=False,
    )
```
